32 devices in a mesh: sec: 4 (over x, core), gy: 4 (over z), gz: 2 (over y).
Axes of the slice: x: 2, y: 2, z: 4, core: 2. Of those that a mesh axis runs over, the one named last changes fastest.
Arguments:
- velocity: float32 [4, 3, 64, 256, 896], P('sec', None, 'gz', 'gy'), may hold values from -6 to 6
- diffusion: float32 [64], P('gz'), may hold values from 0.05 to 0.24
- turbines: int32 [3, 8, 3], replicated, may hold values from 0 to 895, as said below
- fringe_start: int32 [3], replicated, may hold values from 0 to 768
Outputs:
- velocity_out: float32 [4, 3, 64, 256, 896], P('sec', None, 'gz', 'gy')
The draws below stay inside these ranges and needn't reach their ends.
Inputs may be any that keep to these rules, and one draw needn't show every extreme that they name: turbines[f, t] = (x0, y0, z0) with x0 < 896, y0 + 16 <= 256, z0 + 16 <= 64.
All inputs are finite; a program needn't handle non-finite values.
Results may differ from the reference program's by a relative error of at most 0.0003.
Values sent between devices are 32-bit elements; how exact they have to be, the bound alone decides.
A program may use at most 192 MiB of HBM per device.

```python
import math
import jax
import jax.numpy as jnp
from jax import lax

NX = 896
NY = 256
NZ = 64
FRINGE = 128
DISK = 16
NTURB = 8
STEPS = 1
SEC = 4
FARMS = 3


def draw_turbines(key, part):
    subkeys = jax.random.split(jax.random.fold_in(key, 7), 3)
    plane_pos = jax.random.randint(subkeys[0], (FARMS, NTURB), 0, NX)
    span_pos = jax.random.randint(subkeys[1], (FARMS, NTURB), 0, NY - DISK + 1)
    height_pos = jax.random.randint(subkeys[2], (FARMS, NTURB), 0, NZ - DISK + 1)
    return jnp.stack([plane_pos, span_pos, height_pos], axis=-1).astype(jnp.int32)


def block_scale(stream_key, shape, cuts, low, top_value):
    def one(axis_at, shards_of):
        heights = jax.random.uniform(jax.random.fold_in(jax.random.fold_in(stream_key, 6), axis_at), (shards_of,), jnp.float32, low / len(cuts), top_value / len(cuts))
        return jnp.repeat(jnp.exp(heights), shape[axis_at] // shards_of).reshape((-1,) + (1,) * (len(shape) - axis_at - 1))

    loudness = one(*cuts[0])
    for cut in cuts[1:]:
        loudness = loudness * one(*cut)
    return loudness


def gaussian(stream_key, dims, spread, bound, shards=(), kind=jnp.bfloat16):
    drawn = jax.random.normal(stream_key, dims, jnp.float32) * spread
    if len(shards) > 0:
        drawn = block_scale(stream_key, dims, shards, -0.22, 0.18) * drawn
    return jnp.clip(drawn, min=-bound, max=bound).astype(kind)


def setup_inputs(seed: int = 0) -> dict:
    streams_of = jax.random.split(jax.random.key(seed), 5)
    velocity = gaussian(streams_of[0], (SEC, 3, NZ, NY, NX), 1.0, 6.0, ((0, 4), (2, 2), (3, 4)), jnp.float32)
    diffusion = jnp.clip(jnp.exp(math.log(0.24) - 1.5686159 * jax.random.uniform(streams_of[1], (NZ,), jnp.float32) ** block_scale(streams_of[1], (NZ,), ((0, 2),), -0.2, 0.2)), 0.05, 0.24)
    turbines = draw_turbines(jax.random.fold_in(streams_of[4], 71), 0)
    fringe_start = jax.random.randint(streams_of[3], (FARMS,), 0, NX - FRINGE + 1).astype(jnp.int32)
    return dict(velocity=velocity, diffusion=diffusion, turbines=turbines, fringe_start=fringe_start)


time_step = 0.2
thrust_coef = 1.5


def spectral_slope(values, axis_pos, length):
    wavenum = jnp.fft.fftfreq(length) * (2.0 * jnp.pi)
    wavenum = jnp.where(jnp.arange(length) == length // 2, 0.0, wavenum)
    layout = [1] * values.ndim
    layout[axis_pos] = length
    factor = (1j * wavenum).reshape(layout)
    spectrum = jnp.fft.fft(values, axis=axis_pos)
    return jnp.real(jnp.fft.ifft(factor * spectrum, axis=axis_pos)).astype(values.dtype)


def reference(velocity, diffusion, turbines, fringe_start):
    current = velocity
    plane_index = jnp.arange(NX, dtype=jnp.int32)
    for step_index in range(STEPS):
        advanced_all = []
        for section in range(SEC):
            fields = current[section]
            updated = []
            for component in range(3):
                one_field = fields[component]
                along_x = spectral_slope(one_field, 2, NX)
                along_y = spectral_slope(one_field, 1, NY)
                advection = -((1.0 + fields[0]) * along_x + fields[1] * along_y)
                padded = jnp.pad(one_field, ((1, 1), (0, 0), (0, 0)))
                laplace = padded[2:] + padded[:-2] - 2.0 * one_field
                updated.append(one_field + time_step * advection + diffusion[:, None, None] * laplace)
            if section > 0:
                forcing = jnp.zeros_like(fields[0])
                for turbine in range(NTURB):
                    corner = turbines[section - 1, turbine].astype(jnp.int32)
                    anchor = (corner[2], corner[1], corner[0])
                    rotor = lax.dynamic_slice(fields[0], anchor, (DISK, DISK, 1))
                    speed = 1.0 + jnp.sum(rotor) / (DISK * DISK)
                    thrust = -0.5 * thrust_coef * speed * jnp.abs(speed)
                    patch = lax.dynamic_slice(forcing, anchor, (DISK, DISK, 1)) + thrust
                    forcing = lax.dynamic_update_slice(forcing, patch, anchor)
                updated[0] = updated[0] + time_step * forcing
            advanced_all.append(jnp.stack(updated))
        inflow = advanced_all[0][..., NX - FRINGE:]
        blended = [advanced_all[0]]
        for section in range(1, SEC):
            first_plane = fringe_start[section - 1].astype(jnp.int32)
            offset = plane_index - first_plane
            inside = (offset >= 0) & (offset < FRINGE)
            weight = jnp.where(inside, jnp.sin(jnp.pi * (offset.astype(jnp.float32) + 0.5) / FRINGE) ** 2, 0.0)
            placed = lax.dynamic_update_slice_in_dim(jnp.zeros_like(advanced_all[section]), inflow, first_plane, 3)
            blended.append(advanced_all[section] + weight * (placed - advanced_all[section]))
        current = jnp.stack(blended)
    return current
```

```python
import functools

import jax
import jax.numpy as jnp
import numpy as np
from jax import lax
from jax.experimental import pallas as pl
from jax.experimental.pallas import tpu as pltpu
from jax.sharding import PartitionSpec as P

FRINGE = 128
DISK = 16
LANES = 128
RANK = 8
KEEP = 16
LEAD = 3
LAG = 1
SLOTS = 4

time_step = 0.2
thrust_coef = 1.5

MESH = pl.DeviceIdType.MESH


def slope_matrix(n):
    i = np.arange(n)
    d = (i[:, None] - i[None, :]) % n
    safe = np.where(d == 0, 1, d)
    return np.where(d == 0, 0.0, np.pi / n * (1.0 - 2.0 * (d % 2)) / np.tan(safe * np.pi / n))


def leading(matrix, keep):
    basis = np.linalg.svd(matrix, full_matrices=False)[2][:keep].T
    signs = np.sign(basis[np.argmax(np.abs(basis), axis=0), np.arange(basis.shape[1])])
    return np.round(basis * signs * 2.0**25) / 2.0**25


def halves(x):
    x = np.asarray(x, np.float32)
    high = x.astype(jnp.bfloat16)
    return np.stack([high, (x - high.astype(np.float32)).astype(jnp.bfloat16)])


def split(x):
    high = x.astype(jnp.bfloat16)
    return high, (x - high.astype(jnp.float32)).astype(jnp.bfloat16)


def mm(a, b):
    return jnp.dot(a, b, preferred_element_type=jnp.float32)


def ring_factors(matrix, width):
    block = lambda a, b: matrix[(a % 4) * width : (a % 4 + 1) * width, (b % 4) * width : (b % 4 + 1) * width]
    project, merges, applies = [], [], []
    for sign in (1, -1):
        basis = lambda g: leading(np.concatenate([block(g, 0), block(2, 0)], axis=0), RANK)
        held = lambda g: leading(np.concatenate([block(g, 0), block(2, 0)], axis=1).T, RANK)
        own = basis(sign)
        column = held(-sign)
        other = column.T @ block(-sign, 0)
        partner_basis = basis(-sign)
        merge = column.T @ block(2, 0) @ partner_basis
        apply_first = block(0, sign) @ partner_basis
        apply_second = held(sign)
        project.append(np.concatenate([own.T, other], axis=0))
        merges.append(merge)
        applies.append(np.concatenate([block(0, 0), apply_first, apply_second], axis=1))
    return np.stack(project), np.stack(merges), np.stack(applies)


def exchange_kernel(
    sizes, diff_ref, tur_ref, v_hbm, mx_ref, wp_ref, wm_ref, wy_ref,
    adv_hbm, inflow_hbm, rotor_ref,
    v_scr, first_send, first_recv, second_send, second_recv, stage, masks, rot_acc, rot_send, rot_recv,
    load_sem, first_ssem, first_rsem, second_ssem, second_rsem, store_sem, halo_ssem, halo_rsem, flow_ssem, flow_rsem,
    rot_ssem, rot_rsem,
):
    sections, devices, count, zb = sizes
    _, depth, width, length = v_hbm.shape
    units = depth // zb
    turbines = tur_ref.shape[1]
    section, me, gz = lax.axis_index("sec"), lax.axis_index("gy"), lax.axis_index("gz")
    half = length // 2

    barrier = pltpu.get_barrier_semaphore()
    group = [(dy, dz) for dy in range(devices) for dz in range(count) if (dy, dz) != (0, 0)]
    peer = lambda dy, dz: {"gy": (me + dy) % devices, "gz": (gz + dz) % count}
    for dy, dz in group:
        pl.semaphore_signal(barrier, inc=1, device_id=peer(dy, dz), device_id_type=MESH)
    for ds in range(1, sections):
        pl.semaphore_signal(barrier, inc=1, device_id={"sec": (section + ds) % sections}, device_id_type=MESH)

    backward = (gz + count - 1) // count
    unit_of = lambda i: backward * (units - 1 - i) + (1 - backward) * i
    z_of = lambda i: unit_of(i) * zb

    def load(i):
        z0 = z_of(i)
        return pltpu.make_async_copy(v_hbm.at[:, pl.ds(z0, zb)], v_scr.at[:, pl.ds(z0 + 1, zb)], load_sem.at[i])

    @pl.loop(0, units)
    def _(i):
        load(i).start()

    pl.semaphore_wait(barrier, len(group) + sections - 1)

    up = lambda: pltpu.make_async_remote_copy(
        v_hbm.at[:, depth - 1], v_scr.at[:, 0], halo_ssem.at[0], halo_rsem.at[0],
        device_id={"gz": (gz + 1) % count}, device_id_type=MESH,
    )
    down = lambda: pltpu.make_async_remote_copy(
        v_hbm.at[:, 0], v_scr.at[:, depth + 1], halo_ssem.at[1], halo_rsem.at[1],
        device_id={"gz": (gz + count - 1) % count}, device_id_type=MESH,
    )

    @pl.when(gz < count - 1)
    def _():
        up().start()

    @pl.when(gz > 0)
    def _():
        down().start()

    @pl.when(gz == 0)
    def _():
        v_scr[:, 0] = jnp.zeros((3, width, length), jnp.float32)

    @pl.when(gz == count - 1)
    def _():
        v_scr[:, depth + 1] = jnp.zeros((3, width, length), jnp.float32)

    farm_row = (section + sections - 1) % sections % (sections - 1)
    corner = []
    for k in range(3):
        row = lax.broadcasted_iota(jnp.int32, (turbines, LANES), 0)
        got = jnp.zeros((turbines, LANES), jnp.int32)
        for t in range(turbines):
            got = jnp.where(row == t, tur_ref[farm_row, t, k], got)
        corner.append(got)
    ys = me * width + lax.broadcasted_iota(jnp.int32, (turbines, LANES), 1)
    spans = jnp.where((ys >= corner[1]) & (ys < corner[1] + DISK), 1.0, 0.0)
    masks[...] = jnp.concatenate([spans, jnp.zeros((16 - turbines, LANES), jnp.float32)], axis=0).astype(jnp.bfloat16)
    rot_acc[...] = jnp.zeros_like(rot_acc)

    turn = lambda i: (me + i) % 2

    def first_copy(i):
        other = (me + 1 - 2 * turn(i) + devices) % devices
        return pltpu.make_async_remote_copy(
            first_send.at[i], first_recv.at[i], first_ssem.at[i], first_rsem.at[i], device_id={"gy": other}, device_id_type=MESH
        )

    def second_copy(i):
        other = (me - 1 + 2 * turn(i) + devices) % devices
        return pltpu.make_async_remote_copy(
            second_send.at[i], second_recv.at[i], second_ssem.at[i], second_rsem.at[i], device_id={"gy": other}, device_id_type=MESH
        )

    def project(i):
        side, z0 = turn(i), z_of(i)
        wh, wl = wp_ref[side, 0], wp_ref[side, 1]
        for c in range(3):
            for z in range(zb):
                high, low = split(v_scr[c, z0 + 1 + z])
                if c == 0:
                    tall = jnp.concatenate([wh, masks[:, :width]], axis=0)
                    got = mm(tall, high) + mm(tall, low)
                    zs = gz * depth + z0 + z
                    live = jnp.where((zs >= corner[2]) & (zs < corner[2] + DISK), 1.0, 0.0)
                    for q in range(length // LANES):
                        at = slice(q * LANES, (q + 1) * LANES)
                        rot_acc[:, at] += live * got[2 * RANK : 2 * RANK + turbines, at]
                    got = got[: 2 * RANK] + mm(wl, high)
                else:
                    got = mm(wh, high) + mm(wh, low) + mm(wl, high)
                first_send[i, c, z] = got[:RANK]
                second_send[i, c, z] = got[RANK:]

    def merge(i):
        side = turn(i)
        for c in range(3):
            for z in range(zb):
                total = second_send[i, c, z]
                came = first_recv[i, c, z]
                for k in range(RANK):
                    total = total + jnp.concatenate([wm_ref[side, k]] * (length // LANES), axis=1) * came[k : k + 1]
                second_send[i, c, z] = total

    def along(i):
        z0, slot = z_of(i), i % SLOTS
        rows = jnp.concatenate([v_scr[c, pl.ds(z0 + 1, zb)].reshape(zb * width, length) for c in range(3)], axis=0)
        wide = mx_ref.shape[-1]
        ahead = pltpu.roll(rows[:, length - wide :], wide - (half - (length - wide)), 1)
        sides = []
        for g, data in enumerate((rows[:, :wide] + ahead, rows[:, :wide] - ahead)):
            high, low = split(data)
            sides.append(mm(high, mx_ref[g, 0]) + mm(low, mx_ref[g, 0]) + mm(high, mx_ref[g, 1]))
        near, far = sides[0] + sides[1], sides[0] - sides[1]
        back = half % LANES
        far = pltpu.roll(far, back, 1)
        cut = half - back
        lane = lax.broadcasted_iota(jnp.int32, (rows.shape[0], LANES), 1)
        seam = jnp.where(lane < back, near[:, cut : cut + LANES], far[:, :LANES])
        slope = jnp.concatenate([near[:, :cut], seam, far[:, LANES : LANES + length - cut - LANES]], axis=1)
        for c in range(3):
            for z in range(zb):
                here = v_scr[c, z0 + 1 + z]
                at = (c * zb + z) * width
                laplace = v_scr[c, z0 + z] + v_scr[c, z0 + 2 + z] - 2.0 * here
                tendency = (1.0 + v_scr[0, z0 + 1 + z]) * slope[at : at + width]
                stage[slot, c, z] = here - time_step * tendency + diff_ref[z0 + z] * laplace

    def across(i):
        side, z0, slot = turn(i), z_of(i), i % SLOTS
        wh, wl = wy_ref[side, 0], wy_ref[side, 1]
        for z in range(zb):
            speed = v_scr[1, z0 + 1 + z]
            for c in range(3):
                data = jnp.concatenate([v_scr[c, z0 + 1 + z], first_recv[i, c, z], second_recv[i, c, z]], axis=0)
                high, low = split(data)
                slope = mm(wh, high) + mm(wh, low) + mm(wl, high)
                stage[slot, c, z] = stage[slot, c, z] - time_step * (speed * slope)

    def store(i):
        return pltpu.make_async_copy(stage.at[i % SLOTS], adv_hbm.at[:, pl.ds(z_of(i), zb)], store_sem.at[i % SLOTS])

    lanes = pl.ds(length - FRINGE, FRINGE)

    def flow(i, to, sem):
        return pltpu.make_async_remote_copy(
            stage.at[i % SLOTS, :, :, :, lanes], inflow_hbm.at[:, pl.ds(z_of(i), zb)], sem.at[i], flow_rsem.at[i],
            device_id={"sec": to}, device_id_type=MESH,
        )

    def relay(i):
        here = inflow_hbm.at[:, pl.ds(z_of(i), zb)]
        return pltpu.make_async_remote_copy(
            here, here, flow_ssem.at[0, i], flow_rsem.at[i], device_id={"sec": (section + 1) % sections}, device_id_type=MESH
        )

    targets = [to for to in (1, 2) if to < sections]

    def emit(i):
        store(i).start()

        @pl.when(section == 0)
        def _():
            for at, to in enumerate(targets):
                flow(i, to, flow_ssem.at[at]).start()

    def free(i):
        store(i).wait()

        @pl.when(section == 0)
        def _():
            for at, to in enumerate(targets):
                flow(i, to, flow_ssem.at[at]).wait_send()

    def pass_on(i):
        @pl.when(section > 0)
        def _():
            relay(i).wait_recv()

        @pl.when((section > 1) & (section < sections - 1))
        def _():
            relay(i).start()

    def wait_halo(i):
        @pl.when((unit_of(i) == 0) & (gz > 0))
        def _():
            up().wait_recv()

        @pl.when((unit_of(i) == units - 1) & (gz < count - 1))
        def _():
            down().wait_recv()

    def step(i, with_project, with_along, with_across):
        if with_project:
            load(i + LEAD).wait()
        if with_along:
            wait_halo(i)

            @pl.when(i >= SLOTS)
            def _():
                free(i - SLOTS)

        if with_across:
            second_copy(i - LAG).wait_recv()
        if with_project:
            project(i + LEAD)
        if with_along:
            along(i)
        if with_across:
            across(i - LAG)
        if with_project:
            first_copy(i + LEAD).start()
        if with_across:
            emit(i - LAG)
        if with_along:
            first_copy(i).wait_recv()
            merge(i)
            second_copy(i).start()
        if with_across:

            @pl.when(i >= LAG + 2)
            def _():
                pass_on(i - LAG - 2)

    def run(low, high, *flags):
        if high > low:

            @pl.loop(low, high)
            def _(i):
                step(i, *flags)

    run(-LEAD, 0, True, False, False)
    run(0, LAG, True, True, False)
    run(LAG, units - LEAD, True, True, True)

    xs = lax.broadcasted_iota(jnp.int32, (turbines, LANES), 1)
    folded = jnp.zeros((turbines, LANES), jnp.float32)
    for q in range(length // LANES):
        folded = folded + jnp.where(xs + q * LANES == corner[0], rot_acc[:, q * LANES : (q + 1) * LANES], 0.0)
    rot_send[...] = folded
    rotor = lambda at: pltpu.make_async_remote_copy(
        rot_send, rot_recv.at[at], rot_ssem.at[at], rot_rsem.at[at], device_id=peer(*group[at]), device_id_type=MESH
    )

    run(units - LEAD, units - LEAD + 1, False, True, True)
    for at in range(len(group)):
        rotor(at).start()
    run(units - LEAD + 1, units, False, True, True)
    run(units, units + LAG, False, False, True)

    total = rot_send[...]
    for at in range(len(group)):
        rotor(at).wait()
        total = total + rot_recv[at]
    rotor_ref[...] = total

    @pl.when(gz < count - 1)
    def _():
        up().wait_send()

    @pl.when(gz > 0)
    def _():
        down().wait_send()

    @pl.loop(0, units)
    def _(i):
        first_copy(i).wait_send()
        second_copy(i).wait_send()

    for i in range(units - 2, units):
        pass_on(i)
    for i in range(units - SLOTS, units):
        free(i)

    @pl.when((section > 1) & (section < sections - 1))
    def _():
        @pl.loop(0, units)
        def _(i):
            relay(i).wait_send()


def finish_kernel(sections, tur_ref, start_ref, adv_ref, inflow_ref, rotor_ref, out_ref):
    section, me, gz = lax.axis_index("sec"), lax.axis_index("gy"), lax.axis_index("gz")
    _, zb, width, length = adv_ref.shape
    farm = (section + sections - 1) % sections % (sections - 1)
    out_ref[...] = adv_ref[...]

    @pl.when(section > 0)
    def _():
        y0, z0 = me * width, (gz * pl.num_programs(0) + pl.program_id(0)) * zb
        speed = 1.0 + jnp.sum(rotor_ref[...], axis=1, keepdims=True) / (DISK * DISK)
        thrust = -0.5 * thrust_coef * speed * jnp.abs(speed)
        for t in range(tur_ref.shape[1]):
            tx, ty, tz = (tur_ref[farm, t, k] for k in range(3))

            @pl.when((tz < z0 + zb) & (tz + DISK > z0) & (ty < y0 + width) & (ty + DISK > y0))
            def _():
                shape = (zb, width, LANES)
                zs = z0 + lax.broadcasted_iota(jnp.int32, shape, 0)
                ys = y0 + lax.broadcasted_iota(jnp.int32, shape, 1)
                left = pl.multiple_of(tx // LANES * LANES, LANES)
                xs = left + lax.broadcasted_iota(jnp.int32, shape, 2)
                hit = (xs == tx) & (ys >= ty) & (ys < ty + DISK) & (zs >= tz) & (zs < tz + DISK)
                push = (time_step * thrust[t : t + 1]).reshape(1, 1, 1)
                at = pl.ds(left, LANES)
                out_ref[0, :, :, at] = out_ref[0, :, :, at] + jnp.where(hit, push, 0.0)

        start = start_ref[farm]
        turn = lax.rem(start, LANES)
        for j in range(2):

            @pl.when(start // LANES + j < length // LANES)
            def _():
                left = pl.multiple_of((start // LANES + j) * LANES, LANES)
                at = pl.ds(left, LANES)
                offset = left + lax.broadcasted_iota(jnp.int32, (1, LANES), 1) - start
                inside = (offset >= 0) & (offset < FRINGE)
                weight = jnp.where(inside, jnp.sin(jnp.pi * (offset.astype(jnp.float32) + 0.5) / FRINGE) ** 2, 0.0)
                for c in range(3):
                    for z in range(zb):
                        here = out_ref[c, z, :, at]
                        out_ref[c, z, :, at] = here + weight * (pltpu.roll(inflow_ref[c, z], turn, 1) - here)


def cost(flops, bytes_accessed):
    return pl.CostEstimate(flops=int(flops), bytes_accessed=int(bytes_accessed), transcendentals=0)


def ring_body(velocity, diffusion, turbines, fringe_start):
    current = velocity[0]
    _, depth, width, length = current.shape
    sections, devices, count = (lax.axis_size(a) for a in ("sec", "gy", "gz"))
    f32, bf16 = jnp.float32, jnp.bfloat16
    zb = 2
    units = depth // zb
    rows = 3 * depth
    half = length // 2
    wide = -(-half // LANES) * LANES
    number = turbines.shape[1]

    straight = slope_matrix(length)
    mx = np.zeros((2, wide, wide))
    mx[0, :half, :half] = 0.5 * (straight[:half, :half] + straight[:half, half:]).T
    mx[1, :half, :half] = 0.5 * (straight[:half, :half] - straight[:half, half:]).T
    project, merges, applies = ring_factors(slope_matrix(width * devices), width)
    pair = lambda x: np.moveaxis(halves(x), 0, 1)
    wm = np.broadcast_to(np.moveaxis(merges, 2, 1)[..., None], merges.shape + (LANES,)).astype(np.float32)
    consts = [jnp.asarray(x) for x in (pair(mx), pair(project), wm, pair(applies))]

    vmem = pl.BlockSpec(memory_space=pltpu.VMEM)
    smem = pl.BlockSpec(memory_space=pltpu.SMEM)
    hbm = pl.BlockSpec(memory_space=pl.ANY)
    message = pltpu.VMEM((units, 3, zb, RANK, length), f32)
    dma = pltpu.SemaphoreType.DMA
    others = devices * count - 1
    advanced, inflow, rotor = pl.pallas_call(
        functools.partial(exchange_kernel, (sections, devices, count, zb)),
        out_shape=(
            jax.ShapeDtypeStruct(current.shape, f32),
            jax.ShapeDtypeStruct((3, depth, width, FRINGE), f32),
            jax.ShapeDtypeStruct((number, LANES), f32),
        ),
        in_specs=[smem, smem, hbm, vmem, vmem, vmem, vmem],
        out_specs=(hbm, hbm, vmem),
        scratch_shapes=[
            pltpu.VMEM((3, depth + 2, width, length), f32),
            message, message, message, message,
            pltpu.VMEM((SLOTS, 3, zb, width, length), f32),
            pltpu.VMEM((16, LANES), bf16),
            pltpu.VMEM((number, length), f32),
            pltpu.VMEM((number, LANES), f32),
            pltpu.VMEM((others, number, LANES), f32),
            dma((units,)), dma((units,)), dma((units,)), dma((units,)), dma((units,)), dma((SLOTS,)), dma((2,)), dma((2,)),
            dma((2, units)), dma((units,)), dma((others,)), dma((others,)),
        ],
        compiler_params=pltpu.CompilerParams(collective_id=0, has_side_effects=True, vmem_limit_bytes=62 * 1024 * 1024),
        cost_estimate=cost(6 * rows * width * length * length, 12 * rows * width * length),
        name="exchange",
    )(diffusion, turbines, current, *consts)

    zc = min(4, depth)
    out = pl.pallas_call(
        functools.partial(finish_kernel, sections),
        out_shape=jax.ShapeDtypeStruct(current.shape, f32),
        grid_spec=pltpu.PrefetchScalarGridSpec(
            num_scalar_prefetch=2,
            grid=(depth // zc,),
            in_specs=[
                pl.BlockSpec((3, zc, width, length), lambda i, *_: (0, i, 0, 0)),
                pl.BlockSpec((3, zc, width, FRINGE), lambda i, *_: (0, i, 0, 0)),
                pl.BlockSpec((number, LANES), lambda i, *_: (0, 0)),
            ],
            out_specs=pl.BlockSpec((3, zc, width, length), lambda i, *_: (0, i, 0, 0)),
        ),
        compiler_params=pltpu.CompilerParams(dimension_semantics=("arbitrary",), vmem_limit_bytes=40 * 1024 * 1024),
        cost_estimate=cost(rows * width * length, 8 * rows * width * length),
        name="finish",
    )(turbines, fringe_start, advanced, inflow, rotor)
    return out[None]


def gather_body(velocity, diffusion, turbines, fringe_start):
    current = velocity[0]
    _, depth, width, length = current.shape
    sections, devices, count = (lax.axis_size(a) for a in ("sec", "gy", "gz"))
    section, me, gz = (lax.axis_index(a) for a in ("sec", "gy", "gz"))
    f32 = jnp.float32
    matrix = slope_matrix(width * devices)
    block = lambda d: matrix[(d % devices) * width : (d % devices + 1) * width, :width]
    keep = min(KEEP, width)
    basis = leading(np.concatenate([block(d) for d in range(1, devices)], axis=0), keep)
    table = np.stack([np.zeros((width, keep))] + [block(d) @ basis for d in range(1, devices)]).astype(np.float32)
    dot = functools.partial(jnp.einsum, precision=lax.Precision.HIGHEST, preferred_element_type=f32)
    table = jnp.take(jnp.asarray(table), (me - jnp.arange(devices)) % devices, axis=0)

    def advection_of(field):
        coeffs = dot("ky,zyx->zkx", jnp.asarray(basis.T, f32), field)
        gathered = lax.all_gather(coeffs, "gy")
        along_y = dot("ab,zbx->zax", jnp.asarray(matrix[:width, :width], f32), field)
        along_y = along_y + dot("dyk,dzkx->zyx", table, gathered)
        along_x = dot("zyb,ab->zya", field, jnp.asarray(slope_matrix(length), f32))
        return -((1.0 + current[0]) * along_x + current[1] * along_y)

    advection = lax.map(advection_of, current)
    low = lax.ppermute(current[:, -1:], "gz", [(i, i + 1) for i in range(count - 1)])
    high = lax.ppermute(current[:, :1], "gz", [(i + 1, i) for i in range(count - 1)])
    padded = jnp.concatenate([low, current, high], axis=1)
    laplace = padded[:, 2:] + padded[:, :-2] - 2.0 * current
    advanced = current + time_step * advection + diffusion[:, None, None] * laplace

    farm = jnp.maximum(section - 1, 0)
    corners = lax.dynamic_index_in_dim(turbines, farm, 0, keepdims=False)
    zs = (gz * depth + jnp.arange(depth))[:, None, None]
    ys = (me * width + jnp.arange(width))[None, :, None]
    xs = jnp.arange(length)[None, None, :]
    hits = [
        (xs == x) & (ys >= y) & (ys < y + DISK) & (zs >= z) & (zs < z + DISK) for x, y, z in (corners[t] for t in range(corners.shape[0]))
    ]
    sums = lax.psum(jnp.stack([jnp.sum(jnp.where(hit, current[0], 0.0)) for hit in hits]), ("gy", "gz"))
    speed = 1.0 + sums / (DISK * DISK)
    thrust = jnp.where(section > 0, -0.5 * thrust_coef * speed * jnp.abs(speed), 0.0)
    forcing = sum(jnp.where(hit, thrust[t], 0.0) for t, hit in enumerate(hits))
    advanced = advanced.at[0].add(time_step * forcing)

    inflow = lax.psum(jnp.where(section == 0, advanced[..., length - FRINGE :], 0.0), "sec")
    start = lax.dynamic_index_in_dim(fringe_start, farm, 0, keepdims=False)
    offset = jnp.arange(length, dtype=jnp.int32) - start
    inside = (offset >= 0) & (offset < FRINGE) & (section > 0)
    weight = jnp.where(inside, jnp.sin(jnp.pi * (offset.astype(f32) + 0.5) / FRINGE) ** 2, 0.0)
    placed = lax.dynamic_update_slice_in_dim(jnp.zeros_like(advanced), inflow, start, 3)
    return (advanced + weight * (placed - advanced))[None]


def solution(mesh):
    in_specs = (P("sec", None, "gz", "gy", None), P("gz"), P(), P())
    out_specs = P("sec", None, "gz", "gy", None)
    body = ring_body if mesh.shape["gy"] == 4 else gather_body
    return jax.shard_map(body, mesh=mesh, in_specs=in_specs, out_specs=out_specs, check_vma=False)
```

```python
import functools

import jax
import jax.numpy as jnp
import numpy as np
from jax import lax
from jax.experimental import pallas as pl
from jax.experimental.pallas import tpu as pltpu
from jax.sharding import PartitionSpec as P

FRINGE = 128
DISK = 16
LANES = 128
RANK = 8
KEEP = 16
LEAD = 4
AHEAD = 1
LAG = 2
SLOTS = 6

time_step = 0.2
thrust_coef = 1.5

MESH = pl.DeviceIdType.MESH


def slope_matrix(n):
    i = np.arange(n)
    d = (i[:, None] - i[None, :]) % n
    safe = np.where(d == 0, 1, d)
    return np.where(d == 0, 0.0, np.pi / n * (1.0 - 2.0 * (d % 2)) / np.tan(safe * np.pi / n))


def leading(matrix, keep):
    basis = np.linalg.svd(matrix, full_matrices=False)[2][:keep].T
    signs = np.sign(basis[np.argmax(np.abs(basis), axis=0), np.arange(basis.shape[1])])
    return np.round(basis * signs * 2.0**25) / 2.0**25


def halves(x):
    x = np.asarray(x, np.float32)
    high = x.astype(jnp.bfloat16)
    return np.stack([high, (x - high.astype(np.float32)).astype(jnp.bfloat16)])


def split(x):
    high = x.astype(jnp.bfloat16)
    return high, (x - high.astype(jnp.float32)).astype(jnp.bfloat16)


def mm(a, b):
    return jnp.dot(a, b, preferred_element_type=jnp.float32)


def ring_factors(matrix, width):
    block = lambda a, b: matrix[(a % 4) * width : (a % 4 + 1) * width, (b % 4) * width : (b % 4 + 1) * width]
    project, merges, applies = [], [], []
    for sign in (1, -1):
        basis = lambda g: leading(np.concatenate([block(g, 0), block(2, 0)], axis=0), RANK)
        held = lambda g: leading(np.concatenate([block(g, 0), block(2, 0)], axis=1).T, RANK)
        own = basis(sign)
        column = held(-sign)
        other = column.T @ block(-sign, 0)
        partner_basis = basis(-sign)
        merge = column.T @ block(2, 0) @ partner_basis
        apply_first = block(0, sign) @ partner_basis
        apply_second = held(sign)
        project.append(np.concatenate([own.T, other], axis=0))
        merges.append(merge)
        applies.append(np.concatenate([block(0, 0), apply_first, apply_second], axis=1))
    return np.stack(project), np.stack(merges), np.stack(applies)


def exchange_kernel(
    sizes, diff_ref, tur_ref, v_hbm, mx_ref, wp_ref, wm_ref, wy_ref,
    adv_hbm, inflow_hbm, rotor_ref,
    v_scr, first_send, first_recv, second_send, second_recv, stage, masks, rot_acc, rot_send, rot_recv,
    load_sem, first_ssem, first_rsem, second_ssem, second_rsem, store_sem, halo_ssem, halo_rsem, flow_ssem, flow_rsem,
    rot_ssem, rot_rsem,
):
    sections, devices, count, zb = sizes
    _, depth, width, length = v_hbm.shape
    units = depth // zb
    turbines = tur_ref.shape[2]
    section, me, gz = lax.axis_index("sec"), lax.axis_index("gy"), lax.axis_index("gz")
    half = length // 2

    barrier = pltpu.get_barrier_semaphore()
    group = [(dy, dz) for dy in range(devices) for dz in range(count) if (dy, dz) != (0, 0)]
    peer = lambda dy, dz: {"gy": (me + dy) % devices, "gz": (gz + dz) % count}
    for dy, dz in group:
        pl.semaphore_signal(barrier, inc=1, device_id=peer(dy, dz), device_id_type=MESH)
    for ds in range(1, sections):
        pl.semaphore_signal(barrier, inc=1, device_id={"sec": (section + ds) % sections}, device_id_type=MESH)

    backward = (gz + count - 1) // count
    unit_of = lambda i: backward * (units - 1 - i) + (1 - backward) * i
    z_of = lambda i: unit_of(i) * zb

    def load(i):
        z0 = z_of(i)
        return pltpu.make_async_copy(v_hbm.at[:, pl.ds(z0, zb)], v_scr.at[:, pl.ds(z0 + 1, zb)], load_sem.at[i])

    @pl.loop(0, units)
    def _(i):
        load(i).start()

    pl.semaphore_wait(barrier, len(group) + sections - 1)

    up = lambda: pltpu.make_async_remote_copy(
        v_hbm.at[:, depth - 1], v_scr.at[:, 0], halo_ssem.at[0], halo_rsem.at[0],
        device_id={"gz": (gz + 1) % count}, device_id_type=MESH,
    )
    down = lambda: pltpu.make_async_remote_copy(
        v_hbm.at[:, 0], v_scr.at[:, depth + 1], halo_ssem.at[1], halo_rsem.at[1],
        device_id={"gz": (gz + count - 1) % count}, device_id_type=MESH,
    )

    @pl.when(gz < count - 1)
    def _():
        up().start()

    @pl.when(gz > 0)
    def _():
        down().start()

    @pl.when(gz == 0)
    def _():
        v_scr[:, 0] = jnp.zeros((3, width, length), jnp.float32)

    @pl.when(gz == count - 1)
    def _():
        v_scr[:, depth + 1] = jnp.zeros((3, width, length), jnp.float32)

    farm_row = (section + sections - 1) % sections % (sections - 1)
    corner = []
    for k in range(3):
        row = lax.broadcasted_iota(jnp.int32, (turbines, LANES), 0)
        got = jnp.zeros((turbines, LANES), jnp.int32)
        for t in range(turbines):
            got = jnp.where(row == t, tur_ref[farm_row, k, t], got)
        corner.append(got)
    ys = me * width + lax.broadcasted_iota(jnp.int32, (turbines, LANES), 1)
    spans = jnp.where((ys >= corner[1]) & (ys < corner[1] + DISK), 1.0, 0.0)
    masks[...] = jnp.concatenate([spans, jnp.zeros((16 - turbines, LANES), jnp.float32)], axis=0).astype(jnp.bfloat16)
    rot_acc[...] = jnp.zeros_like(rot_acc)

    turn = lambda i: (me + i) % 2

    def first_copy(i):
        other = (me + 1 - 2 * turn(i) + devices) % devices
        return pltpu.make_async_remote_copy(
            first_send.at[i], first_recv.at[i], first_ssem.at[i], first_rsem.at[i], device_id={"gy": other}, device_id_type=MESH
        )

    def second_copy(i):
        other = (me - 1 + 2 * turn(i) + devices) % devices
        return pltpu.make_async_remote_copy(
            second_send.at[i], second_recv.at[i], second_ssem.at[i], second_rsem.at[i], device_id={"gy": other}, device_id_type=MESH
        )

    def project(i):
        side, z0 = turn(i), z_of(i)
        wh, wl = wp_ref[side, 0], wp_ref[side, 1]
        for c in range(3):
            for z in range(zb):
                high, low = split(v_scr[c, z0 + 1 + z])
                if c == 0:
                    tall = jnp.concatenate([wh, masks[:, :width]], axis=0)
                    got = mm(tall, high) + mm(tall, low)
                    zs = gz * depth + z0 + z
                    live = jnp.where((zs >= corner[2]) & (zs < corner[2] + DISK), 1.0, 0.0)
                    for q in range(length // LANES):
                        at = slice(q * LANES, (q + 1) * LANES)
                        rot_acc[:, at] += live * got[2 * RANK : 2 * RANK + turbines, at]
                    got = got[: 2 * RANK] + mm(wl, high)
                else:
                    got = mm(wh, high) + mm(wh, low) + mm(wl, high)
                first_send[i, c, z] = got[:RANK]
                second_send[i, c, z] = got[RANK:]

    def merge(i):
        side = turn(i)
        for c in range(3):
            for z in range(zb):
                total = second_send[i, c, z]
                came = first_recv[i, c, z]
                for k in range(RANK):
                    total = total + jnp.concatenate([wm_ref[side, k]] * (length // LANES), axis=1) * came[k : k + 1]
                second_send[i, c, z] = total

    def along(i):
        z0, slot = z_of(i), i % SLOTS
        rows = jnp.concatenate([v_scr[c, pl.ds(z0 + 1, zb)].reshape(zb * width, length) for c in range(3)], axis=0)
        wide = mx_ref.shape[-1]
        ahead = pltpu.roll(rows[:, length - wide :], wide - (half - (length - wide)), 1)
        sides = []
        for g, data in enumerate((rows[:, :wide] + ahead, rows[:, :wide] - ahead)):
            high, low = split(data)
            sides.append(mm(high, mx_ref[g, 0]) + mm(low, mx_ref[g, 0]) + mm(high, mx_ref[g, 1]))
        near, far = sides[0] + sides[1], sides[0] - sides[1]
        back = half % LANES
        far = pltpu.roll(far, back, 1)
        cut = half - back
        lane = lax.broadcasted_iota(jnp.int32, (rows.shape[0], LANES), 1)
        seam = jnp.where(lane < back, near[:, cut : cut + LANES], far[:, :LANES])
        slope = jnp.concatenate([near[:, :cut], seam, far[:, LANES : LANES + length - cut - LANES]], axis=1)
        for c in range(3):
            for z in range(zb):
                here = v_scr[c, z0 + 1 + z]
                at = (c * zb + z) * width
                laplace = v_scr[c, z0 + z] + v_scr[c, z0 + 2 + z] - 2.0 * here
                tendency = (1.0 + v_scr[0, z0 + 1 + z]) * slope[at : at + width]
                stage[slot, c, z] = here - time_step * tendency + diff_ref[z0 + z] * laplace

    def across(i):
        side, z0, slot = turn(i), z_of(i), i % SLOTS
        wh, wl = wy_ref[side, 0], wy_ref[side, 1]
        for z in range(zb):
            speed = v_scr[1, z0 + 1 + z]
            for c in range(3):
                data = jnp.concatenate([v_scr[c, z0 + 1 + z], first_recv[i, c, z], second_recv[i, c, z]], axis=0)
                high, low = split(data)
                slope = mm(wh, high) + mm(wh, low) + mm(wl, high)
                stage[slot, c, z] = stage[slot, c, z] - time_step * (speed * slope)

    def store(i):
        return pltpu.make_async_copy(stage.at[i % SLOTS], adv_hbm.at[:, pl.ds(z_of(i), zb)], store_sem.at[i % SLOTS])

    lanes = pl.ds(length - FRINGE, FRINGE)

    def flow(i, to, sem):
        return pltpu.make_async_remote_copy(
            stage.at[i % SLOTS, :, :, :, lanes], inflow_hbm.at[:, pl.ds(z_of(i), zb)], sem.at[i], flow_rsem.at[i],
            device_id={"sec": to}, device_id_type=MESH,
        )

    def relay(i):
        here = inflow_hbm.at[:, pl.ds(z_of(i), zb)]
        return pltpu.make_async_remote_copy(
            here, here, flow_ssem.at[0, i], flow_rsem.at[i], device_id={"sec": (section + 1) % sections}, device_id_type=MESH
        )

    targets = [to for to in (1, 2) if to < sections]

    def emit(i):
        store(i).start()

        @pl.when(section == 0)
        def _():
            for at, to in enumerate(targets):
                flow(i, to, flow_ssem.at[at]).start()

    def free(i):
        store(i).wait()

        @pl.when(section == 0)
        def _():
            for at, to in enumerate(targets):
                flow(i, to, flow_ssem.at[at]).wait_send()

    def pass_on(i):
        @pl.when(section > 0)
        def _():
            relay(i).wait_recv()

        @pl.when((section > 1) & (section < sections - 1))
        def _():
            relay(i).start()

    def wait_halo(i):
        @pl.when((unit_of(i) == 0) & (gz > 0))
        def _():
            up().wait_recv()

        @pl.when((unit_of(i) == units - 1) & (gz < count - 1))
        def _():
            down().wait_recv()

    def forward(i):
        first_copy(i).wait_recv()
        merge(i)
        second_copy(i).start()

    def step(i, with_project, with_along, with_across):
        if with_project:
            load(i + LEAD).wait()
        if with_along:
            wait_halo(i)

            @pl.when(i >= SLOTS)
            def _():
                free(i - SLOTS)

        if with_across:
            second_copy(i - LAG).wait_recv()
        if with_project:
            project(i + LEAD)
        if with_along:
            along(i)
        if with_across:
            across(i - LAG)
        if with_project:
            first_copy(i + LEAD).start()
        if with_across:
            emit(i - LAG)
        if with_along:

            @pl.when(i == 0)
            def _():
                @pl.loop(0, AHEAD)
                def _(j):
                    forward(j)

            @pl.when(i < units - AHEAD)
            def _():
                forward(i + AHEAD)

        if with_across:

            @pl.when(i >= LAG + 2)
            def _():
                pass_on(i - LAG - 2)

    def run(low, high, *flags):
        if high > low:

            @pl.loop(low, high)
            def _(i):
                step(i, *flags)

    run(-LEAD, 0, True, False, False)
    run(0, LAG, True, True, False)
    run(LAG, units - LEAD, True, True, True)

    xs = lax.broadcasted_iota(jnp.int32, (turbines, LANES), 1)
    folded = jnp.zeros((turbines, LANES), jnp.float32)
    for q in range(length // LANES):
        folded = folded + jnp.where(xs + q * LANES == corner[0], rot_acc[:, q * LANES : (q + 1) * LANES], 0.0)
    rot_send[...] = folded
    rotor = lambda at: pltpu.make_async_remote_copy(
        rot_send, rot_recv.at[at], rot_ssem.at[at], rot_rsem.at[at], device_id=peer(*group[at]), device_id_type=MESH
    )

    run(units - LEAD, units - LEAD + 1, False, True, True)
    for at in range(len(group)):
        rotor(at).start()
    run(units - LEAD + 1, units, False, True, True)
    run(units, units + LAG, False, False, True)

    total = rot_send[...]
    for at in range(len(group)):
        rotor(at).wait()
        total = total + rot_recv[at]
    rotor_ref[...] = total

    @pl.when(gz < count - 1)
    def _():
        up().wait_send()

    @pl.when(gz > 0)
    def _():
        down().wait_send()

    @pl.loop(0, units)
    def _(i):
        first_copy(i).wait_send()
        second_copy(i).wait_send()

    for i in range(units - 2, units):
        pass_on(i)
    for i in range(units - SLOTS, units):
        free(i)

    @pl.when((section > 1) & (section < sections - 1))
    def _():
        @pl.loop(0, units)
        def _(i):
            relay(i).wait_send()


def finish_kernel(sections, tur_ref, start_ref, adv_ref, inflow_ref, rotor_ref, out_ref):
    section, me, gz = lax.axis_index("sec"), lax.axis_index("gy"), lax.axis_index("gz")
    _, zb, width, length = adv_ref.shape
    farm = (section + sections - 1) % sections % (sections - 1)
    out_ref[...] = adv_ref[...]

    @pl.when(section > 0)
    def _():
        y0, z0 = me * width, (gz * pl.num_programs(0) + pl.program_id(0)) * zb
        speed = 1.0 + jnp.sum(rotor_ref[...], axis=1, keepdims=True) / (DISK * DISK)
        thrust = -0.5 * thrust_coef * speed * jnp.abs(speed)
        for t in range(tur_ref.shape[2]):
            tx, ty, tz = (tur_ref[farm, k, t] for k in range(3))

            @pl.when((tz < z0 + zb) & (tz + DISK > z0) & (ty < y0 + width) & (ty + DISK > y0))
            def _():
                shape = (zb, width, LANES)
                zs = z0 + lax.broadcasted_iota(jnp.int32, shape, 0)
                ys = y0 + lax.broadcasted_iota(jnp.int32, shape, 1)
                left = pl.multiple_of(tx // LANES * LANES, LANES)
                xs = left + lax.broadcasted_iota(jnp.int32, shape, 2)
                hit = (xs == tx) & (ys >= ty) & (ys < ty + DISK) & (zs >= tz) & (zs < tz + DISK)
                push = (time_step * thrust[t : t + 1]).reshape(1, 1, 1)
                at = pl.ds(left, LANES)
                out_ref[0, :, :, at] = out_ref[0, :, :, at] + jnp.where(hit, push, 0.0)

        start = start_ref[farm]
        turn = lax.rem(start, LANES)
        for j in range(2):

            @pl.when(start // LANES + j < length // LANES)
            def _():
                left = pl.multiple_of((start // LANES + j) * LANES, LANES)
                at = pl.ds(left, LANES)
                offset = left + lax.broadcasted_iota(jnp.int32, (1, LANES), 1) - start
                inside = (offset >= 0) & (offset < FRINGE)
                weight = jnp.where(inside, jnp.sin(jnp.pi * (offset.astype(jnp.float32) + 0.5) / FRINGE) ** 2, 0.0)
                for c in range(3):
                    for z in range(zb):
                        here = out_ref[c, z, :, at]
                        out_ref[c, z, :, at] = here + weight * (pltpu.roll(inflow_ref[c, z], turn, 1) - here)


def cost(flops, bytes_accessed):
    return pl.CostEstimate(flops=int(flops), bytes_accessed=int(bytes_accessed), transcendentals=0)


def ring_body(velocity, diffusion, turbines, fringe_start):
    current = velocity[0]
    _, depth, width, length = current.shape
    sections, devices, count = (lax.axis_size(a) for a in ("sec", "gy", "gz"))
    f32, bf16 = jnp.float32, jnp.bfloat16
    zb = 2
    units = depth // zb
    rows = 3 * depth
    half = length // 2
    wide = -(-half // LANES) * LANES
    number = turbines.shape[1]
    turbines = jnp.swapaxes(turbines, 1, 2)

    straight = slope_matrix(length)
    mx = np.zeros((2, wide, wide))
    mx[0, :half, :half] = 0.5 * (straight[:half, :half] + straight[:half, half:]).T
    mx[1, :half, :half] = 0.5 * (straight[:half, :half] - straight[:half, half:]).T
    project, merges, applies = ring_factors(slope_matrix(width * devices), width)
    pair = lambda x: np.moveaxis(halves(x), 0, 1)
    wm = np.broadcast_to(np.moveaxis(merges, 2, 1)[..., None], merges.shape + (LANES,)).astype(np.float32)
    consts = [jnp.asarray(x) for x in (pair(mx), pair(project), wm, pair(applies))]

    vmem = pl.BlockSpec(memory_space=pltpu.VMEM)
    smem = pl.BlockSpec(memory_space=pltpu.SMEM)
    hbm = pl.BlockSpec(memory_space=pl.ANY)
    message = pltpu.VMEM((units, 3, zb, RANK, length), f32)
    dma = pltpu.SemaphoreType.DMA
    others = devices * count - 1
    advanced, inflow, rotor = pl.pallas_call(
        functools.partial(exchange_kernel, (sections, devices, count, zb)),
        out_shape=(
            jax.ShapeDtypeStruct(current.shape, f32),
            jax.ShapeDtypeStruct((3, depth, width, FRINGE), f32),
            jax.ShapeDtypeStruct((number, LANES), f32),
        ),
        in_specs=[smem, smem, hbm, vmem, vmem, vmem, vmem],
        out_specs=(hbm, hbm, vmem),
        scratch_shapes=[
            pltpu.VMEM((3, depth + 2, width, length), f32),
            message, message, message, message,
            pltpu.VMEM((SLOTS, 3, zb, width, length), f32),
            pltpu.VMEM((16, LANES), bf16),
            pltpu.VMEM((number, length), f32),
            pltpu.VMEM((number, LANES), f32),
            pltpu.VMEM((others, number, LANES), f32),
            dma((units,)), dma((units,)), dma((units,)), dma((units,)), dma((units,)), dma((SLOTS,)), dma((2,)), dma((2,)),
            dma((2, units)), dma((units,)), dma((others,)), dma((others,)),
        ],
        compiler_params=pltpu.CompilerParams(collective_id=0, has_side_effects=True, vmem_limit_bytes=62 * 1024 * 1024),
        cost_estimate=cost(6 * rows * width * length * length, 12 * rows * width * length),
        name="exchange",
    )(diffusion, turbines, current, *consts)

    zc = min(2, depth)
    out = pl.pallas_call(
        functools.partial(finish_kernel, sections),
        out_shape=jax.ShapeDtypeStruct(current.shape, f32),
        grid_spec=pltpu.PrefetchScalarGridSpec(
            num_scalar_prefetch=2,
            grid=(depth // zc,),
            in_specs=[
                pl.BlockSpec((3, zc, width, length), lambda i, *_: (0, i, 0, 0)),
                pl.BlockSpec((3, zc, width, FRINGE), lambda i, *_: (0, i, 0, 0)),
                pl.BlockSpec((number, LANES), lambda i, *_: (0, 0)),
            ],
            out_specs=pl.BlockSpec((3, zc, width, length), lambda i, *_: (0, i, 0, 0)),
        ),
        compiler_params=pltpu.CompilerParams(dimension_semantics=("arbitrary",), vmem_limit_bytes=62 * 1024 * 1024),
        cost_estimate=cost(rows * width * length, 8 * rows * width * length),
        name="finish",
    )(turbines, fringe_start, advanced, inflow, rotor)
    return out[None]


def gather_body(velocity, diffusion, turbines, fringe_start):
    current = velocity[0]
    _, depth, width, length = current.shape
    sections, devices, count = (lax.axis_size(a) for a in ("sec", "gy", "gz"))
    section, me, gz = (lax.axis_index(a) for a in ("sec", "gy", "gz"))
    f32 = jnp.float32
    matrix = slope_matrix(width * devices)
    block = lambda d: matrix[(d % devices) * width : (d % devices + 1) * width, :width]
    keep = min(KEEP, width)
    basis = leading(np.concatenate([block(d) for d in range(1, devices)], axis=0), keep)
    table = np.stack([np.zeros((width, keep))] + [block(d) @ basis for d in range(1, devices)]).astype(np.float32)
    dot = functools.partial(jnp.einsum, precision=lax.Precision.HIGHEST, preferred_element_type=f32)
    table = jnp.take(jnp.asarray(table), (me - jnp.arange(devices)) % devices, axis=0)

    def advection_of(field):
        coeffs = dot("ky,zyx->zkx", jnp.asarray(basis.T, f32), field)
        gathered = lax.all_gather(coeffs, "gy")
        along_y = dot("ab,zbx->zax", jnp.asarray(matrix[:width, :width], f32), field)
        along_y = along_y + dot("dyk,dzkx->zyx", table, gathered)
        along_x = dot("zyb,ab->zya", field, jnp.asarray(slope_matrix(length), f32))
        return -((1.0 + current[0]) * along_x + current[1] * along_y)

    advection = lax.map(advection_of, current)
    low = lax.ppermute(current[:, -1:], "gz", [(i, i + 1) for i in range(count - 1)])
    high = lax.ppermute(current[:, :1], "gz", [(i + 1, i) for i in range(count - 1)])
    padded = jnp.concatenate([low, current, high], axis=1)
    laplace = padded[:, 2:] + padded[:, :-2] - 2.0 * current
    advanced = current + time_step * advection + diffusion[:, None, None] * laplace

    farm = jnp.maximum(section - 1, 0)
    corners = lax.dynamic_index_in_dim(turbines, farm, 0, keepdims=False)
    zs = (gz * depth + jnp.arange(depth))[:, None, None]
    ys = (me * width + jnp.arange(width))[None, :, None]
    xs = jnp.arange(length)[None, None, :]
    hits = [
        (xs == x) & (ys >= y) & (ys < y + DISK) & (zs >= z) & (zs < z + DISK) for x, y, z in (corners[t] for t in range(corners.shape[0]))
    ]
    sums = lax.psum(jnp.stack([jnp.sum(jnp.where(hit, current[0], 0.0)) for hit in hits]), ("gy", "gz"))
    speed = 1.0 + sums / (DISK * DISK)
    thrust = jnp.where(section > 0, -0.5 * thrust_coef * speed * jnp.abs(speed), 0.0)
    forcing = sum(jnp.where(hit, thrust[t], 0.0) for t, hit in enumerate(hits))
    advanced = advanced.at[0].add(time_step * forcing)

    inflow = lax.psum(jnp.where(section == 0, advanced[..., length - FRINGE :], 0.0), "sec")
    start = lax.dynamic_index_in_dim(fringe_start, farm, 0, keepdims=False)
    offset = jnp.arange(length, dtype=jnp.int32) - start
    inside = (offset >= 0) & (offset < FRINGE) & (section > 0)
    weight = jnp.where(inside, jnp.sin(jnp.pi * (offset.astype(f32) + 0.5) / FRINGE) ** 2, 0.0)
    placed = lax.dynamic_update_slice_in_dim(jnp.zeros_like(advanced), inflow, start, 3)
    return (advanced + weight * (placed - advanced))[None]


def solution(mesh):
    in_specs = (P("sec", None, "gz", "gy", None), P("gz"), P(), P())
    out_specs = P("sec", None, "gz", "gy", None)
    body = ring_body if mesh.shape["gy"] == 4 else gather_body
    return jax.shard_map(body, mesh=mesh, in_specs=in_specs, out_specs=out_specs, check_vma=False)
```

```python
import functools

import jax
import jax.numpy as jnp
import numpy as np
from jax import lax
from jax.experimental import pallas as pl
from jax.experimental.pallas import tpu as pltpu
from jax.sharding import PartitionSpec as P

FRINGE = 128
DISK = 16
LANES = 128
RANK = 12
TILE = 8
HEIGHTS = 2
LAG = 1
SLOTS = 4

time_step = 0.2
thrust_coef = 1.5

MESH = pl.DeviceIdType.MESH


def slope_matrix(n):
    i = np.arange(n)
    d = (i[:, None] - i[None, :]) % n
    safe = np.where(d == 0, 1, d)
    return np.where(d == 0, 0.0, np.pi / n * (1.0 - 2.0 * (d % 2)) / np.tan(safe * np.pi / n))


def leading(matrix, keep):
    basis = np.linalg.svd(matrix)[2][:keep].T
    signs = np.sign(basis[np.argmax(np.abs(basis), axis=0), np.arange(basis.shape[1])])
    return np.round(basis * signs * 2.0**25) / 2.0**25


def halves(x):
    x = np.asarray(x, np.float32)
    high = x.astype(jnp.bfloat16)
    return np.stack([high, (x - high.astype(np.float32)).astype(jnp.bfloat16)])


def split(x):
    high = x.astype(jnp.bfloat16)
    return high, (x - high.astype(jnp.float32)).astype(jnp.bfloat16)


def mm(a, b):
    return jnp.dot(a, b, preferred_element_type=jnp.float32)


def line_factors(matrix, devices, order):
    width = matrix.shape[0] // devices
    block = lambda a, b: matrix[a * width : (a + 1) * width, b * width : (b + 1) * width]
    own = np.zeros((devices, RANK, width))
    merge = np.zeros((devices, RANK, RANK))
    apply = np.zeros((devices, width, RANK))
    before = None
    for at, here in enumerate(order):
        if before is not None:
            apply[here] = before[:width]
            before = before[width:]
        ahead = order[at + 1 :]
        if not ahead:
            continue
        rows = np.concatenate([np.concatenate([block(a, b) for b in order[: at + 1]], axis=1) for a in ahead], axis=0)
        held = leading(rows.T, RANK)
        own[here] = held.T @ rows[:, at * width :]
        if before is not None:
            merge[here] = held.T @ before
        before = held
    return own, merge, apply


def flow_factors(matrix, devices):
    width = matrix.shape[0] // devices
    rest = RANK - TILE
    place = np.zeros((HEIGHTS, 3 * TILE, RANK))
    for z in range(HEIGHTS):
        place[z, z * TILE : (z + 1) * TILE, :TILE] = np.eye(TILE)
        place[z, 2 * TILE + z * rest : 2 * TILE + (z + 1) * rest, TILE:] = np.eye(rest)
    project = np.zeros((devices, HEIGHTS, 4 * TILE, width))
    merges = np.zeros((devices, 2, 3 * TILE, 3 * TILE))
    applies = np.zeros((devices, HEIGHTS, width, width + 4 * TILE))
    applies[..., :width] = matrix[:width, :width]
    for f, order in enumerate((list(range(devices)), list(range(devices))[::-1])):
        own, merge, apply = line_factors(matrix, devices, order)
        for z in range(HEIGHTS):
            spread = np.concatenate([place[z, z * TILE : (z + 1) * TILE], place[z, 2 * TILE :]], axis=0)
            project[:, z, 2 * f * TILE : 2 * (f + 1) * TILE] = spread @ own
            merges[:, f] += place[z] @ merge @ place[z].T
            applies[:, z, :, width + 2 * f * TILE : width + 2 * (f + 1) * TILE] = apply @ spread.T
    return project, merges, applies


def exchange_kernel(
    sizes, diff_ref, tur_ref, v_hbm, mx_ref, wp_ref, wm_ref, wy_ref,
    adv_hbm, inflow_hbm, rotor_ref,
    v_scr, send_r, recv_r, send_l, recv_l, stage, masks, rot_acc, rot_send, rot_recv,
    load_sem, ssem_r, rsem_r, ssem_l, rsem_l, store_sem, halo_ssem, halo_rsem, flow_ssem, flow_rsem,
    rot_ssem, rot_rsem,
):
    sections, devices, count, lead, hop = sizes
    zb = HEIGHTS
    _, depth, width, length = v_hbm.shape
    units = depth // zb
    turbines = tur_ref.shape[2]
    section, me, gz = lax.axis_index("sec"), lax.axis_index("gy"), lax.axis_index("gz")
    half = length // 2

    barrier = pltpu.get_barrier_semaphore()
    group = [(dy, dz) for dy in range(devices) for dz in range(count) if (dy, dz) != (0, 0)]
    peer = lambda dy, dz: {"gy": (me + dy) % devices, "gz": (gz + dz) % count}
    for dy, dz in group:
        pl.semaphore_signal(barrier, inc=1, device_id=peer(dy, dz), device_id_type=MESH)
    for ds in range(1, sections):
        pl.semaphore_signal(barrier, inc=1, device_id={"sec": (section + ds) % sections}, device_id_type=MESH)

    backward = (gz + count - 1) // count
    unit_of = lambda i: backward * (units - 1 - i) + (1 - backward) * i
    z_of = lambda i: unit_of(i) * zb

    def load(i):
        z0 = z_of(i)
        return pltpu.make_async_copy(v_hbm.at[:, pl.ds(z0, zb)], v_scr.at[:, pl.ds(z0 + 1, zb)], load_sem.at[i])

    @pl.loop(0, units)
    def _(i):
        load(i).start()

    pl.semaphore_wait(barrier, len(group) + sections - 1)

    up = lambda: pltpu.make_async_remote_copy(
        v_hbm.at[:, depth - 1], v_scr.at[:, 0], halo_ssem.at[0], halo_rsem.at[0],
        device_id={"gz": (gz + 1) % count}, device_id_type=MESH,
    )
    down = lambda: pltpu.make_async_remote_copy(
        v_hbm.at[:, 0], v_scr.at[:, depth + 1], halo_ssem.at[1], halo_rsem.at[1],
        device_id={"gz": (gz + count - 1) % count}, device_id_type=MESH,
    )

    @pl.when(gz < count - 1)
    def _():
        up().start()

    @pl.when(gz > 0)
    def _():
        down().start()

    @pl.when(gz == 0)
    def _():
        v_scr[:, 0] = jnp.zeros((3, width, length), jnp.float32)

    @pl.when(gz == count - 1)
    def _():
        v_scr[:, depth + 1] = jnp.zeros((3, width, length), jnp.float32)

    farm_row = (section + sections - 1) % sections % (sections - 1)
    corner = []
    for k in range(3):
        row = lax.broadcasted_iota(jnp.int32, (turbines, LANES), 0)
        got = jnp.zeros((turbines, LANES), jnp.int32)
        for t in range(turbines):
            got = jnp.where(row == t, tur_ref[farm_row, k, t], got)
        corner.append(got)
    ys = me * width + lax.broadcasted_iota(jnp.int32, (turbines, LANES), 1)
    spans = jnp.where((ys >= corner[1]) & (ys < corner[1] + DISK), 1.0, 0.0)
    masks[...] = jnp.concatenate([spans, jnp.zeros((16 - turbines, LANES), jnp.float32)], axis=0).astype(jnp.bfloat16)
    rot_acc[...] = jnp.zeros_like(rot_acc)

    flows = (
        (me, 1, send_r, recv_r, ssem_r, rsem_r),
        (devices - 1 - me, devices - 1, send_l, recv_l, ssem_l, rsem_l),
    )
    for place, _, _, came, _, _ in flows:

        @pl.when(place == 0)
        def _():
            @pl.loop(0, units)
            def _(i):
                came[i] = jnp.zeros(came.shape[1:], jnp.float32)

    def message(f, i, c):
        _, step, sent, came, ssem, rsem = flows[f]
        return pltpu.make_async_remote_copy(
            sent.at[i, c], came.at[i, c], ssem.at[i, c], rsem.at[i, c],
            device_id={"gy": (me + step) % devices}, device_id_type=MESH,
        )

    def project(i):
        z0 = z_of(i)
        for c in range(3):
            rests = []
            for z in range(zb):
                wh, wl = wp_ref[me, z, 0], wp_ref[me, z, 1]
                high, low = split(v_scr[c, z0 + 1 + z])
                if c == 0:
                    tall = jnp.concatenate([wh, masks[:, :width]], axis=0)
                    got = mm(tall, high) + mm(tall, low)
                    zs = gz * depth + z0 + z
                    live = jnp.where((zs >= corner[2]) & (zs < corner[2] + DISK), 1.0, 0.0)
                    for q in range(length // LANES):
                        at = slice(q * LANES, (q + 1) * LANES)
                        rot_acc[:, at] += live * got[4 * TILE : 4 * TILE + turbines, at]
                    got = got[: 4 * TILE] + mm(wl, high)
                else:
                    got = mm(wh, high) + mm(wh, low) + mm(wl, high)
                send_r[i, c, z] = got[:TILE]
                send_l[i, c, z] = got[2 * TILE : 3 * TILE]
                rests.append((got[TILE : 2 * TILE], got[3 * TILE :]))
            send_r[i, c, 2] = rests[0][0] + rests[1][0]
            send_l[i, c, 2] = rests[0][1] + rests[1][1]

    def forward(f, q):
        place, _, sent, came, _, _ = flows[f]
        i, c = q // 3, q % 3

        @pl.when((q >= 0) & (q < 3 * units))
        def _():
            @pl.when(place > 0)
            def _():
                message(f, i, c).wait_recv()

            @pl.when((place > 0) & (place < devices - 1))
            def _():
                high, low = split(came[i, c].reshape(3 * TILE, length))
                wh, wl = wm_ref[me, f, 0], wm_ref[me, f, 1]
                got = mm(wh, high) + mm(wh, low) + mm(wl, high)
                sent[i, c] = sent[i, c] + got.reshape(3, TILE, length)

            @pl.when(place < devices - 1)
            def _():
                message(f, i, c).start()

    def relays(i):
        for k in range(3):
            for f in range(2):
                forward(f, 3 * (i + lead) + k - hop * flows[f][0])

    def along(i):
        z0, slot = z_of(i), i % SLOTS
        rows = jnp.concatenate([v_scr[c, pl.ds(z0 + 1, zb)].reshape(zb * width, length) for c in range(3)], axis=0)
        wide = mx_ref.shape[-1]
        ahead = pltpu.roll(rows[:, length - wide :], wide - (half - (length - wide)), 1)
        sides = []
        for g, data in enumerate((rows[:, :wide] + ahead, rows[:, :wide] - ahead)):
            high, low = split(data)
            sides.append(mm(high, mx_ref[g, 0]) + mm(low, mx_ref[g, 0]) + mm(high, mx_ref[g, 1]))
        near, far = sides[0] + sides[1], sides[0] - sides[1]
        back = half % LANES
        far = pltpu.roll(far, back, 1)
        cut = half - back
        lane = lax.broadcasted_iota(jnp.int32, (rows.shape[0], LANES), 1)
        seam = jnp.where(lane < back, near[:, cut : cut + LANES], far[:, :LANES])
        slope = jnp.concatenate([near[:, :cut], seam, far[:, LANES : LANES + length - cut - LANES]], axis=1)
        for c in range(3):
            for z in range(zb):
                here = v_scr[c, z0 + 1 + z]
                at = (c * zb + z) * width
                laplace = v_scr[c, z0 + z] + v_scr[c, z0 + 2 + z] - 2.0 * here
                tendency = (1.0 + v_scr[0, z0 + 1 + z]) * slope[at : at + width]
                stage[slot, c, z] = here - time_step * tendency + diff_ref[z0 + z] * laplace

    def across(i):
        z0, slot = z_of(i), i % SLOTS
        for z in range(zb):
            wh, wl = wy_ref[me, z, 0], wy_ref[me, z, 1]
            speed = v_scr[1, z0 + 1 + z]
            for c in range(3):
                parts = [v_scr[c, z0 + 1 + z], recv_r[i, c, z], recv_r[i, c, 2], recv_l[i, c, z], recv_l[i, c, 2]]
                high, low = split(jnp.concatenate(parts, axis=0))
                slope = mm(wh, high) + mm(wh, low) + mm(wl, high)
                stage[slot, c, z] = stage[slot, c, z] - time_step * (speed * slope)

    def store(i):
        return pltpu.make_async_copy(stage.at[i % SLOTS], adv_hbm.at[:, pl.ds(z_of(i), zb)], store_sem.at[i % SLOTS])

    lanes = pl.ds(length - FRINGE, FRINGE)

    def flow(i, to, sem):
        return pltpu.make_async_remote_copy(
            stage.at[i % SLOTS, :, :, :, lanes], inflow_hbm.at[:, pl.ds(z_of(i), zb)], sem.at[i], flow_rsem.at[i],
            device_id={"sec": to}, device_id_type=MESH,
        )

    def relay(i):
        here = inflow_hbm.at[:, pl.ds(z_of(i), zb)]
        return pltpu.make_async_remote_copy(
            here, here, flow_ssem.at[0, i], flow_rsem.at[i], device_id={"sec": (section + 1) % sections}, device_id_type=MESH
        )

    targets = [to for to in (1, 2) if to < sections]

    def emit(i):
        store(i).start()

        @pl.when(section == 0)
        def _():
            for at, to in enumerate(targets):
                flow(i, to, flow_ssem.at[at]).start()

    def free(i):
        store(i).wait()

        @pl.when(section == 0)
        def _():
            for at, to in enumerate(targets):
                flow(i, to, flow_ssem.at[at]).wait_send()

    def pass_on(i):
        @pl.when(section > 0)
        def _():
            relay(i).wait_recv()

        @pl.when((section > 1) & (section < sections - 1))
        def _():
            relay(i).start()

    def wait_halo(i):
        @pl.when((unit_of(i) == 0) & (gz > 0))
        def _():
            up().wait_recv()

        @pl.when((unit_of(i) == units - 1) & (gz < count - 1))
        def _():
            down().wait_recv()

    def step(i, with_project, with_along, with_across):
        if with_project:
            load(i + lead).wait()
        if with_along:
            wait_halo(i)

            @pl.when(i >= SLOTS)
            def _():
                free(i - SLOTS)

        if with_project:
            project(i + lead)
        if not with_across or with_along:
            relays(i)
        if with_along:
            along(i)
        if with_along and not with_project:
            rotor_sums(i)
        if with_across:
            across(i - LAG)
            emit(i - LAG)

            @pl.when(i >= LAG + 2)
            def _():
                pass_on(i - LAG - 2)

    def run(low, high, *flags):
        if high > low:

            @pl.loop(low, high)
            def _(i):
                step(i, *flags)

    rotor = lambda at: pltpu.make_async_remote_copy(
        rot_send, rot_recv.at[at], rot_ssem.at[at], rot_rsem.at[at], device_id=peer(*group[at]), device_id_type=MESH
    )

    def rotor_sums(i):
        @pl.when(i == units - lead)
        def _():
            xs = lax.broadcasted_iota(jnp.int32, (turbines, LANES), 1)
            folded = jnp.zeros((turbines, LANES), jnp.float32)
            for q in range(length // LANES):
                folded = folded + jnp.where(xs + q * LANES == corner[0], rot_acc[:, q * LANES : (q + 1) * LANES], 0.0)
            rot_send[...] = folded

        @pl.when(i == units - lead + 1)
        def _():
            for at in range(len(group)):
                rotor(at).start()

    run(-lead, 0, True, False, False)
    run(0, LAG, True, True, False)
    run(LAG, units - lead, True, True, True)
    run(units - lead, units, False, True, True)
    run(units, units + LAG, False, False, True)

    total = rot_send[...]
    for at in range(len(group)):
        rotor(at).wait()
        total = total + rot_recv[at]
    rotor_ref[...] = total

    @pl.when(gz < count - 1)
    def _():
        up().wait_send()

    @pl.when(gz > 0)
    def _():
        down().wait_send()

    for f in range(2):

        @pl.when(flows[f][0] < devices - 1)
        def _():
            @pl.loop(0, units)
            def _(i):
                for c in range(3):
                    message(f, i, c).wait_send()

    for i in range(units - 2, units):
        pass_on(i)
    for i in range(units - SLOTS, units):
        free(i)

    @pl.when((section > 1) & (section < sections - 1))
    def _():
        @pl.loop(0, units)
        def _(i):
            relay(i).wait_send()


def finish_kernel(sections, tur_ref, start_ref, adv_ref, inflow_ref, rotor_ref, out_ref):
    section, me, gz = lax.axis_index("sec"), lax.axis_index("gy"), lax.axis_index("gz")
    _, zb, width, length = adv_ref.shape
    farm = (section + sections - 1) % sections % (sections - 1)
    out_ref[...] = adv_ref[...]

    @pl.when(section > 0)
    def _():
        y0, z0 = me * width, (gz * pl.num_programs(0) + pl.program_id(0)) * zb
        speed = 1.0 + jnp.sum(rotor_ref[...], axis=1, keepdims=True) / (DISK * DISK)
        thrust = -0.5 * thrust_coef * speed * jnp.abs(speed)
        for t in range(tur_ref.shape[2]):
            tx, ty, tz = (tur_ref[farm, k, t] for k in range(3))

            @pl.when((tz < z0 + zb) & (tz + DISK > z0) & (ty < y0 + width) & (ty + DISK > y0))
            def _():
                shape = (zb, width, LANES)
                zs = z0 + lax.broadcasted_iota(jnp.int32, shape, 0)
                ys = y0 + lax.broadcasted_iota(jnp.int32, shape, 1)
                left = pl.multiple_of(tx // LANES * LANES, LANES)
                xs = left + lax.broadcasted_iota(jnp.int32, shape, 2)
                hit = (xs == tx) & (ys >= ty) & (ys < ty + DISK) & (zs >= tz) & (zs < tz + DISK)
                push = (time_step * thrust[t : t + 1]).reshape(1, 1, 1)
                at = pl.ds(left, LANES)
                out_ref[0, :, :, at] = out_ref[0, :, :, at] + jnp.where(hit, push, 0.0)

        start = start_ref[farm]
        turn = lax.rem(start, LANES)
        for j in range(2):

            @pl.when(start // LANES + j < length // LANES)
            def _():
                left = pl.multiple_of((start // LANES + j) * LANES, LANES)
                at = pl.ds(left, LANES)
                offset = left + lax.broadcasted_iota(jnp.int32, (1, LANES), 1) - start
                inside = (offset >= 0) & (offset < FRINGE)
                weight = jnp.where(inside, jnp.sin(jnp.pi * (offset.astype(jnp.float32) + 0.5) / FRINGE) ** 2, 0.0)
                for c in range(3):
                    for z in range(zb):
                        here = out_ref[c, z, :, at]
                        out_ref[c, z, :, at] = here + weight * (pltpu.roll(inflow_ref[c, z], turn, 1) - here)


def cost(flops, bytes_accessed):
    return pl.CostEstimate(flops=int(flops), bytes_accessed=int(bytes_accessed), transcendentals=0)


def body(velocity, diffusion, turbines, fringe_start):
    current = velocity[0]
    _, depth, width, length = current.shape
    sections, devices, count = (lax.axis_size(a) for a in ("sec", "gy", "gz"))
    f32, bf16 = jnp.float32, jnp.bfloat16
    units = depth // HEIGHTS
    hop = max(1, 12 // (devices - 1))
    lead = -(-hop * (devices - 1) // 3)
    rows = 3 * depth
    half = length // 2
    wide = -(-half // LANES) * LANES
    number = turbines.shape[1]
    turbines = jnp.swapaxes(turbines, 1, 2)

    straight = slope_matrix(length)
    mx = np.zeros((2, wide, wide))
    mx[0, :half, :half] = 0.5 * (straight[:half, :half] + straight[:half, half:]).T
    mx[1, :half, :half] = 0.5 * (straight[:half, :half] - straight[:half, half:]).T
    factors = flow_factors(slope_matrix(width * devices), devices)
    pair = lambda x: np.moveaxis(halves(x), 0, -3)
    consts = [jnp.asarray(pair(x)) for x in (mx, *factors)]

    vmem = pl.BlockSpec(memory_space=pltpu.VMEM)
    smem = pl.BlockSpec(memory_space=pltpu.SMEM)
    hbm = pl.BlockSpec(memory_space=pl.ANY)
    message = pltpu.VMEM((units, 3, 3, TILE, length), f32)
    dma = pltpu.SemaphoreType.DMA
    others = devices * count - 1
    advanced, inflow, rotor = pl.pallas_call(
        functools.partial(exchange_kernel, (sections, devices, count, lead, hop)),
        out_shape=(
            jax.ShapeDtypeStruct(current.shape, f32),
            jax.ShapeDtypeStruct((3, depth, width, FRINGE), f32),
            jax.ShapeDtypeStruct((number, LANES), f32),
        ),
        in_specs=[smem, smem, hbm, vmem, vmem, vmem, vmem],
        out_specs=(hbm, hbm, vmem),
        scratch_shapes=[
            pltpu.VMEM((3, depth + 2, width, length), f32),
            message, message, message, message,
            pltpu.VMEM((SLOTS, 3, HEIGHTS, width, length), f32),
            pltpu.VMEM((16, LANES), bf16),
            pltpu.VMEM((number, length), f32),
            pltpu.VMEM((number, LANES), f32),
            pltpu.VMEM((others, number, LANES), f32),
            dma((units,)), dma((units, 3)), dma((units, 3)), dma((units, 3)), dma((units, 3)), dma((SLOTS,)), dma((2,)), dma((2,)),
            dma((2, units)), dma((units,)), dma((others,)), dma((others,)),
        ],
        compiler_params=pltpu.CompilerParams(collective_id=0, has_side_effects=True, vmem_limit_bytes=62 * 1024 * 1024),
        cost_estimate=cost(6 * rows * width * length * length, 12 * rows * width * length),
        name="exchange",
    )(diffusion, turbines, current, *consts)

    zc = min(8, depth)
    out = pl.pallas_call(
        functools.partial(finish_kernel, sections),
        out_shape=jax.ShapeDtypeStruct(current.shape, f32),
        grid_spec=pltpu.PrefetchScalarGridSpec(
            num_scalar_prefetch=2,
            grid=(depth // zc,),
            in_specs=[
                pl.BlockSpec((3, zc, width, length), lambda i, *_: (0, i, 0, 0)),
                pl.BlockSpec((3, zc, width, FRINGE), lambda i, *_: (0, i, 0, 0)),
                pl.BlockSpec((number, LANES), lambda i, *_: (0, 0)),
            ],
            out_specs=pl.BlockSpec((3, zc, width, length), lambda i, *_: (0, i, 0, 0)),
        ),
        compiler_params=pltpu.CompilerParams(dimension_semantics=("arbitrary",), vmem_limit_bytes=62 * 1024 * 1024),
        cost_estimate=cost(rows * width * length, 8 * rows * width * length),
        name="finish",
    )(turbines, fringe_start, advanced, inflow, rotor)
    return out[None]


def solution(mesh):
    in_specs = (P("sec", None, "gz", "gy", None), P("gz"), P(), P())
    out_specs = P("sec", None, "gz", "gy", None)
    return jax.shard_map(body, mesh=mesh, in_specs=in_specs, out_specs=out_specs, check_vma=False)
```

```python
import functools

import jax
import jax.numpy as jnp
import numpy as np
from jax import lax
from jax.experimental import pallas as pl
from jax.experimental.pallas import tpu as pltpu
from jax.sharding import PartitionSpec as P

FRINGE = 128
DISK = 16
LANES = 128
RANK = 12
TILE = 8
HEIGHTS = 2
LAG = 1
SLOTS = 2

time_step = 0.2
thrust_coef = 1.5

MESH = pl.DeviceIdType.MESH


def slope_matrix(n):
    i = np.arange(n)
    d = (i[:, None] - i[None, :]) % n
    safe = np.where(d == 0, 1, d)
    return np.where(d == 0, 0.0, np.pi / n * (1.0 - 2.0 * (d % 2)) / np.tan(safe * np.pi / n))


def leading(matrix, keep):
    basis = np.linalg.svd(matrix)[2][:keep].T
    signs = np.sign(basis[np.argmax(np.abs(basis), axis=0), np.arange(basis.shape[1])])
    return np.round(basis * signs * 2.0**25) / 2.0**25


def halves(x):
    x = np.asarray(x, np.float32)
    high = x.astype(jnp.bfloat16)
    return np.stack([high, (x - high.astype(np.float32)).astype(jnp.bfloat16)])


def split(x):
    high = x.astype(jnp.bfloat16)
    return high, (x - high.astype(jnp.float32)).astype(jnp.bfloat16)


def mm(a, b):
    return jnp.dot(a, b, preferred_element_type=jnp.float32)


def line_factors(matrix, devices, order):
    width = matrix.shape[0] // devices
    block = lambda a, b: matrix[a * width : (a + 1) * width, b * width : (b + 1) * width]
    own = np.zeros((devices, RANK, width))
    merge = np.zeros((devices, RANK, RANK))
    apply = np.zeros((devices, width, RANK))
    before = None
    for at, here in enumerate(order):
        if before is not None:
            apply[here] = before[:width]
            before = before[width:]
        ahead = order[at + 1 :]
        if not ahead:
            continue
        rows = np.concatenate([np.concatenate([block(a, b) for b in order[: at + 1]], axis=1) for a in ahead], axis=0)
        held = leading(rows.T, RANK)
        own[here] = held.T @ rows[:, at * width :]
        if before is not None:
            merge[here] = held.T @ before
        before = held
    return own, merge, apply


def flow_factors(matrix, devices):
    width = matrix.shape[0] // devices
    rest = RANK - TILE
    place = np.zeros((HEIGHTS, 3 * TILE, RANK))
    for z in range(HEIGHTS):
        place[z, z * TILE : (z + 1) * TILE, :TILE] = np.eye(TILE)
        place[z, 2 * TILE + z * rest : 2 * TILE + (z + 1) * rest, TILE:] = np.eye(rest)
    project = np.zeros((devices, HEIGHTS, 4 * TILE, width))
    merges = np.zeros((devices, 2, 3 * TILE, 3 * TILE))
    applies = np.zeros((devices, HEIGHTS, width, width + 4 * TILE))
    applies[..., :width] = matrix[:width, :width]
    for f, order in enumerate((list(range(devices)), list(range(devices))[::-1])):
        own, merge, apply = line_factors(matrix, devices, order)
        for z in range(HEIGHTS):
            spread = np.concatenate([place[z, z * TILE : (z + 1) * TILE], place[z, 2 * TILE :]], axis=0)
            project[:, z, 2 * f * TILE : 2 * (f + 1) * TILE] = spread @ own
            merges[:, f] += place[z] @ merge @ place[z].T
            applies[:, z, :, width + 2 * f * TILE : width + 2 * (f + 1) * TILE] = apply @ spread.T
    return project, merges, applies


def exchange_kernel(
    sizes, diff_ref, tur_ref, v_hbm, mx_ref, wp_ref, wm_ref, wy_ref,
    v_scr, inflow_ref, rotor_ref,
    send_r, recv_r, send_l, recv_l, stage, masks, rot_acc, rot_send, rot_recv,
    load_sem, ssem_r, rsem_r, ssem_l, rsem_l, halo_ssem, halo_rsem, flow_ssem, flow_rsem,
    rot_ssem, rot_rsem,
):
    sections, devices, count, lead, hop = sizes
    zb = HEIGHTS
    _, depth, width, length = v_hbm.shape
    units = depth // zb
    turbines = tur_ref.shape[2]
    section, me, gz = lax.axis_index("sec"), lax.axis_index("gy"), lax.axis_index("gz")
    half = length // 2

    barrier = pltpu.get_barrier_semaphore()
    group = [(dy, dz) for dy in range(devices) for dz in range(count) if (dy, dz) != (0, 0)]
    peer = lambda dy, dz: {"gy": (me + dy) % devices, "gz": (gz + dz) % count}
    for dy, dz in group:
        pl.semaphore_signal(barrier, inc=1, device_id=peer(dy, dz), device_id_type=MESH)
    for ds in range(1, sections):
        pl.semaphore_signal(barrier, inc=1, device_id={"sec": (section + ds) % sections}, device_id_type=MESH)

    backward = (gz + count - 1) // count
    unit_of = lambda i: backward * (units - 1 - i) + (1 - backward) * i
    z_of = lambda i: unit_of(i) * zb

    def load(i):
        z0 = z_of(i)
        return pltpu.make_async_copy(v_hbm.at[:, pl.ds(z0, zb)], v_scr.at[:, pl.ds(z0 + 1, zb)], load_sem.at[i])

    @pl.loop(0, units)
    def _(i):
        load(i).start()

    pl.semaphore_wait(barrier, len(group) + sections - 1)

    up = lambda: pltpu.make_async_remote_copy(
        v_hbm.at[:, depth - 1], v_scr.at[:, 0], halo_ssem.at[0], halo_rsem.at[0],
        device_id={"gz": (gz + 1) % count}, device_id_type=MESH,
    )
    down = lambda: pltpu.make_async_remote_copy(
        v_hbm.at[:, 0], v_scr.at[:, depth + 1], halo_ssem.at[1], halo_rsem.at[1],
        device_id={"gz": (gz + count - 1) % count}, device_id_type=MESH,
    )

    @pl.when(gz < count - 1)
    def _():
        up().start()

    @pl.when(gz > 0)
    def _():
        down().start()

    @pl.when(gz == 0)
    def _():
        v_scr[:, 0] = jnp.zeros((3, width, length), jnp.float32)

    @pl.when(gz == count - 1)
    def _():
        v_scr[:, depth + 1] = jnp.zeros((3, width, length), jnp.float32)

    farm_row = (section + sections - 1) % sections % (sections - 1)
    corner = []
    for k in range(3):
        row = lax.broadcasted_iota(jnp.int32, (turbines, LANES), 0)
        got = jnp.zeros((turbines, LANES), jnp.int32)
        for t in range(turbines):
            got = jnp.where(row == t, tur_ref[farm_row, k, t], got)
        corner.append(got)
    ys = me * width + lax.broadcasted_iota(jnp.int32, (turbines, LANES), 1)
    spans = jnp.where((ys >= corner[1]) & (ys < corner[1] + DISK), 1.0, 0.0)
    masks[...] = jnp.concatenate([spans, jnp.zeros((16 - turbines, LANES), jnp.float32)], axis=0).astype(jnp.bfloat16)
    rot_acc[...] = jnp.zeros_like(rot_acc)

    flows = (
        (me, 1, send_r, recv_r, ssem_r, rsem_r),
        (devices - 1 - me, devices - 1, send_l, recv_l, ssem_l, rsem_l),
    )
    for place, _, _, came, _, _ in flows:

        @pl.when(place == 0)
        def _():
            @pl.loop(0, units)
            def _(i):
                came[i] = jnp.zeros(came.shape[1:], jnp.float32)

    def message(f, i, c):
        _, step, sent, came, ssem, rsem = flows[f]
        return pltpu.make_async_remote_copy(
            sent.at[i, c], came.at[i, c], ssem.at[i, c], rsem.at[i, c],
            device_id={"gy": (me + step) % devices}, device_id_type=MESH,
        )

    def project(i):
        z0 = z_of(i)
        for c in range(3):
            rests = []
            for z in range(zb):
                wh, wl = wp_ref[me, z, 0], wp_ref[me, z, 1]
                high, low = split(v_scr[c, z0 + 1 + z])
                if c == 0:
                    tall = jnp.concatenate([wh, masks[:, :width]], axis=0)
                    got = mm(tall, high) + mm(tall, low)
                    zs = gz * depth + z0 + z
                    live = jnp.where((zs >= corner[2]) & (zs < corner[2] + DISK), 1.0, 0.0)
                    for q in range(length // LANES):
                        at = slice(q * LANES, (q + 1) * LANES)
                        rot_acc[:, at] += live * got[4 * TILE : 4 * TILE + turbines, at]
                    got = got[: 4 * TILE] + mm(wl, high)
                else:
                    got = mm(wh, high) + mm(wh, low) + mm(wl, high)
                send_r[i, c, z] = got[:TILE]
                send_l[i, c, z] = got[2 * TILE : 3 * TILE]
                rests.append((got[TILE : 2 * TILE], got[3 * TILE :]))
            send_r[i, c, 2] = rests[0][0] + rests[1][0]
            send_l[i, c, 2] = rests[0][1] + rests[1][1]

    def forward(f, q):
        place, _, sent, came, _, _ = flows[f]
        i, c = q // 3, q % 3

        @pl.when((q >= 0) & (q < 3 * units))
        def _():
            @pl.when(place > 0)
            def _():
                message(f, i, c).wait_recv()

            @pl.when((place > 0) & (place < devices - 1))
            def _():
                high, low = split(came[i, c].reshape(3 * TILE, length))
                wh, wl = wm_ref[me, f, 0], wm_ref[me, f, 1]
                got = mm(wh, high) + mm(wh, low) + mm(wl, high)
                sent[i, c] = sent[i, c] + got.reshape(3, TILE, length)

            @pl.when(place < devices - 1)
            def _():
                message(f, i, c).start()

    def relay(i, k):
        for f in range(2):
            forward(f, 3 * (i + lead) + k - hop * flows[f][0])

    def along(i):
        z0, slot = z_of(i), i % SLOTS
        rows = jnp.concatenate([v_scr[c, pl.ds(z0 + 1, zb)].reshape(zb * width, length) for c in range(3)], axis=0)
        wide = mx_ref.shape[-1]
        ahead = pltpu.roll(rows[:, length - wide :], wide - (half - (length - wide)), 1)
        sides = []
        for g, data in enumerate((rows[:, :wide] + ahead, rows[:, :wide] - ahead)):
            high, low = split(data)
            sides.append(mm(high, mx_ref[g, 0]) + mm(low, mx_ref[g, 0]) + mm(high, mx_ref[g, 1]))
        near, far = sides[0] + sides[1], sides[0] - sides[1]
        back = half % LANES
        far = pltpu.roll(far, back, 1)
        cut = half - back
        lane = lax.broadcasted_iota(jnp.int32, (rows.shape[0], LANES), 1)
        seam = jnp.where(lane < back, near[:, cut : cut + LANES], far[:, :LANES])
        slope = jnp.concatenate([near[:, :cut], seam, far[:, LANES : LANES + length - cut - LANES]], axis=1)
        for c in range(3):
            for z in range(zb):
                here = v_scr[c, z0 + 1 + z]
                at = (c * zb + z) * width
                laplace = v_scr[c, z0 + z] + v_scr[c, z0 + 2 + z] - 2.0 * here
                tendency = (1.0 + v_scr[0, z0 + 1 + z]) * slope[at : at + width]
                stage[slot, c, z] = here - time_step * tendency + diff_ref[z0 + z] * laplace

    def across(i):
        z0, slot = z_of(i), i % SLOTS
        for z in range(zb):
            wh, wl = wy_ref[me, z, 0], wy_ref[me, z, 1]
            speed = v_scr[1, z0 + 1 + z]
            for c in range(3):
                parts = [v_scr[c, z0 + 1 + z], recv_r[i, c, z], recv_r[i, c, 2], recv_l[i, c, z], recv_l[i, c, 2]]
                high, low = split(jnp.concatenate(parts, axis=0))
                slope = mm(wh, high) + mm(wh, low) + mm(wl, high)
                v_scr[c, z0 + 1 + z] = stage[slot, c, z] - time_step * (speed * slope)

    lanes = pl.ds(length - FRINGE, FRINGE)

    def flow(i, to):
        z0 = z_of(i)
        return pltpu.make_async_remote_copy(
            v_scr.at[:, pl.ds(z0 + 1, zb), :, lanes], inflow_ref.at[:, pl.ds(z0, zb)], flow_ssem.at[to - 1, i], flow_rsem.at[i],
            device_id={"sec": to}, device_id_type=MESH,
        )

    def emit(i):
        @pl.when(section == 0)
        def _():
            for to in range(1, sections):
                flow(i, to).start()

    def wait_halo(i):
        @pl.when((unit_of(i) == 0) & (gz > 0))
        def _():
            up().wait_recv()

        @pl.when((unit_of(i) == units - 1) & (gz < count - 1))
        def _():
            down().wait_recv()

    def step(i, with_project, with_along, with_across):
        if with_project:
            load(i + lead).wait()
        if with_along:
            wait_halo(i)
        if with_project:
            project(i + lead)
        if with_project or with_along:
            relay(i, 0)
        if with_along:
            along(i)
        if with_along and not with_project:
            rotor_sums(i)
        if with_project or with_along:
            relay(i, 1)
        if with_across:
            across(i - LAG)
            emit(i - LAG)
        if with_project or with_along:
            relay(i, 2)

    def run(low, high, *flags):
        if high > low:

            @pl.loop(low, high)
            def _(i):
                step(i, *flags)

    rotor = lambda at: pltpu.make_async_remote_copy(
        rot_send, rot_recv.at[at], rot_ssem.at[at], rot_rsem.at[at], device_id=peer(*group[at]), device_id_type=MESH
    )

    def rotor_sums(i):
        @pl.when(i == units - lead)
        def _():
            xs = lax.broadcasted_iota(jnp.int32, (turbines, LANES), 1)
            folded = jnp.zeros((turbines, LANES), jnp.float32)
            for q in range(length // LANES):
                folded = folded + jnp.where(xs + q * LANES == corner[0], rot_acc[:, q * LANES : (q + 1) * LANES], 0.0)
            rot_send[...] = folded

        @pl.when(i == units - lead + 1)
        def _():
            for at in range(len(group)):
                rotor(at).start()

    run(-lead, 0, True, False, False)
    run(0, LAG, True, True, False)
    run(LAG, units - lead, True, True, True)
    run(units - lead, units, False, True, True)
    run(units, units + LAG, False, False, True)

    total = rot_send[...]
    for at in range(len(group)):
        rotor(at).wait()
        total = total + rot_recv[at]
    rotor_ref[...] = total

    @pl.when(gz < count - 1)
    def _():
        up().wait_send()

    @pl.when(gz > 0)
    def _():
        down().wait_send()

    for f in range(2):

        @pl.when(flows[f][0] < devices - 1)
        def _():
            @pl.loop(0, units)
            def _(i):
                for c in range(3):
                    message(f, i, c).wait_send()

    @pl.when(section == 0)
    def _():
        @pl.loop(0, units)
        def _(i):
            for to in range(1, sections):
                flow(i, to).wait_send()

    @pl.when(section > 0)
    def _():
        @pl.loop(0, units)
        def _(i):
            flow(i, 1).wait_recv()


def finish_kernel(sections, tur_ref, start_ref, adv_ref, inflow_ref, rotor_ref, out_ref):
    section, me, gz = lax.axis_index("sec"), lax.axis_index("gy"), lax.axis_index("gz")
    _, zb, width, length = out_ref.shape
    base = pl.program_id(0) * zb
    farm = (section + sections - 1) % sections % (sections - 1)
    out_ref[...] = adv_ref[:, pl.ds(base + 1, zb)]

    @pl.when(section > 0)
    def _():
        y0, z0 = me * width, (gz * pl.num_programs(0) + pl.program_id(0)) * zb
        speed = 1.0 + jnp.sum(rotor_ref[...], axis=1, keepdims=True) / (DISK * DISK)
        thrust = -0.5 * thrust_coef * speed * jnp.abs(speed)
        for t in range(tur_ref.shape[2]):
            tx, ty, tz = (tur_ref[farm, k, t] for k in range(3))

            @pl.when((tz < z0 + zb) & (tz + DISK > z0) & (ty < y0 + width) & (ty + DISK > y0))
            def _():
                shape = (zb, width, LANES)
                zs = z0 + lax.broadcasted_iota(jnp.int32, shape, 0)
                ys = y0 + lax.broadcasted_iota(jnp.int32, shape, 1)
                left = pl.multiple_of(tx // LANES * LANES, LANES)
                xs = left + lax.broadcasted_iota(jnp.int32, shape, 2)
                hit = (xs == tx) & (ys >= ty) & (ys < ty + DISK) & (zs >= tz) & (zs < tz + DISK)
                push = (time_step * thrust[t : t + 1]).reshape(1, 1, 1)
                at = pl.ds(left, LANES)
                out_ref[0, :, :, at] = out_ref[0, :, :, at] + jnp.where(hit, push, 0.0)

        start = start_ref[farm]
        turn = lax.rem(start, LANES)
        for j in range(2):

            @pl.when(start // LANES + j < length // LANES)
            def _():
                left = pl.multiple_of((start // LANES + j) * LANES, LANES)
                at = pl.ds(left, LANES)
                offset = left + lax.broadcasted_iota(jnp.int32, (1, LANES), 1) - start
                inside = (offset >= 0) & (offset < FRINGE)
                weight = jnp.where(inside, jnp.sin(jnp.pi * (offset.astype(jnp.float32) + 0.5) / FRINGE) ** 2, 0.0)
                for c in range(3):
                    for z in range(zb):
                        here = out_ref[c, z, :, at]
                        out_ref[c, z, :, at] = here + weight * (pltpu.roll(inflow_ref[c, base + z], turn, 1) - here)


def cost(flops, bytes_accessed):
    return pl.CostEstimate(flops=int(flops), bytes_accessed=int(bytes_accessed), transcendentals=0)


def body(velocity, diffusion, turbines, fringe_start):
    current = velocity[0]
    _, depth, width, length = current.shape
    sections, devices, count = (lax.axis_size(a) for a in ("sec", "gy", "gz"))
    f32, bf16 = jnp.float32, jnp.bfloat16
    units = depth // HEIGHTS
    hop = max(1, 12 // (devices - 1))
    lead = -(-hop * (devices - 1) // 3)
    rows = 3 * depth
    half = length // 2
    wide = -(-half // LANES) * LANES
    number = turbines.shape[1]
    turbines = jnp.swapaxes(turbines, 1, 2)

    straight = slope_matrix(length)
    mx = np.zeros((2, wide, wide))
    mx[0, :half, :half] = 0.5 * (straight[:half, :half] + straight[:half, half:]).T
    mx[1, :half, :half] = 0.5 * (straight[:half, :half] - straight[:half, half:]).T
    factors = flow_factors(slope_matrix(width * devices), devices)
    pair = lambda x: np.moveaxis(halves(x), 0, -3)
    consts = [jnp.asarray(pair(x)) for x in (mx, *factors)]

    vmem = pl.BlockSpec(memory_space=pltpu.VMEM)
    smem = pl.BlockSpec(memory_space=pltpu.SMEM)
    hbm = pl.BlockSpec(memory_space=pl.ANY)
    message = pltpu.VMEM((units, 3, 3, TILE, length), f32)
    dma = pltpu.SemaphoreType.DMA
    others = devices * count - 1
    advanced, inflow, rotor = pl.pallas_call(
        functools.partial(exchange_kernel, (sections, devices, count, lead, hop)),
        out_shape=(
            pltpu.VMEM((3, depth + 2, width, length), f32),
            pltpu.VMEM((3, depth, width, FRINGE), f32),
            pltpu.VMEM((number, LANES), f32),
        ),
        in_specs=[smem, smem, hbm, vmem, vmem, vmem, vmem],
        out_specs=(vmem, vmem, vmem),
        scratch_shapes=[
            message, message, message, message,
            pltpu.VMEM((SLOTS, 3, HEIGHTS, width, length), f32),
            pltpu.VMEM((16, LANES), bf16),
            pltpu.VMEM((number, length), f32),
            pltpu.VMEM((number, LANES), f32),
            pltpu.VMEM((others, number, LANES), f32),
            dma((units,)), dma((units, 3)), dma((units, 3)), dma((units, 3)), dma((units, 3)), dma((2,)), dma((2,)),
            dma((sections - 1, units)), dma((units,)), dma((others,)), dma((others,)),
        ],
        compiler_params=pltpu.CompilerParams(collective_id=0, has_side_effects=True, vmem_limit_bytes=30 * 1024 * 1024),
        cost_estimate=cost(6 * rows * width * length * length, 12 * rows * width * length),
        name="exchange",
    )(diffusion, turbines, current, *consts)

    zc = min(4, depth)
    out = pl.pallas_call(
        functools.partial(finish_kernel, sections),
        out_shape=jax.ShapeDtypeStruct(current.shape, f32),
        grid_spec=pltpu.PrefetchScalarGridSpec(
            num_scalar_prefetch=2,
            grid=(depth // zc,),
            in_specs=[
                vmem, vmem, vmem,
            ],
            out_specs=pl.BlockSpec((3, zc, width, length), lambda i, *_: (0, i, 0, 0)),
        ),
        compiler_params=pltpu.CompilerParams(dimension_semantics=("arbitrary",), vmem_limit_bytes=30 * 1024 * 1024),
        cost_estimate=cost(rows * width * length, 8 * rows * width * length),
        name="finish",
    )(turbines, fringe_start, *(pltpu.with_memory_space_constraint(x, pltpu.VMEM) for x in (advanced, inflow, rotor)))
    return out[None]


def solution(mesh):
    in_specs = (P("sec", None, "gz", "gy", None), P("gz"), P(), P())
    out_specs = P("sec", None, "gz", "gy", None)
    return jax.shard_map(body, mesh=mesh, in_specs=in_specs, out_specs=out_specs, check_vma=False)
```

```python
import functools

import jax
import jax.numpy as jnp
import numpy as np
from jax import lax
from jax.experimental import pallas as pl
from jax.experimental.pallas import tpu as pltpu
from jax.sharding import PartitionSpec as P

FRINGE = 128
DISK = 16
LANES = 128
RANK = 12
TILE = 8
HEIGHTS = 2
LAG = 1
SLOTS = 2

time_step = 0.2
thrust_coef = 1.5

MESH = pl.DeviceIdType.MESH


def slope_matrix(n):
    i = np.arange(n)
    d = (i[:, None] - i[None, :]) % n
    safe = np.where(d == 0, 1, d)
    return np.where(d == 0, 0.0, np.pi / n * (1.0 - 2.0 * (d % 2)) / np.tan(safe * np.pi / n))


def leading(matrix, keep):
    basis = np.linalg.svd(matrix)[2][:keep].T
    signs = np.sign(basis[np.argmax(np.abs(basis), axis=0), np.arange(basis.shape[1])])
    return np.round(basis * signs * 2.0**25) / 2.0**25


def halves(x):
    x = np.asarray(x, np.float32)
    high = x.astype(jnp.bfloat16)
    return np.stack([high, (x - high.astype(np.float32)).astype(jnp.bfloat16)])


def split(x):
    high = x.astype(jnp.bfloat16)
    return high, (x - high.astype(jnp.float32)).astype(jnp.bfloat16)


def mm(a, b):
    return jnp.dot(a, b, preferred_element_type=jnp.float32)


def line_factors(matrix, devices, order):
    width = matrix.shape[0] // devices
    block = lambda a, b: matrix[a * width : (a + 1) * width, b * width : (b + 1) * width]
    own = np.zeros((devices, RANK, width))
    merge = np.zeros((devices, RANK, RANK))
    apply = np.zeros((devices, width, RANK))
    before = None
    for at, here in enumerate(order):
        if before is not None:
            apply[here] = before[:width]
            before = before[width:]
        ahead = order[at + 1 :]
        if not ahead:
            continue
        rows = np.concatenate([np.concatenate([block(a, b) for b in order[: at + 1]], axis=1) for a in ahead], axis=0)
        held = leading(rows.T, RANK)
        own[here] = held.T @ rows[:, at * width :]
        if before is not None:
            merge[here] = held.T @ before
        before = held
    return own, merge, apply


def flow_factors(matrix, devices):
    width = matrix.shape[0] // devices
    rest = RANK - TILE
    place = np.zeros((HEIGHTS, 3 * TILE, RANK))
    for z in range(HEIGHTS):
        place[z, z * TILE : (z + 1) * TILE, :TILE] = np.eye(TILE)
        place[z, 2 * TILE + z * rest : 2 * TILE + (z + 1) * rest, TILE:] = np.eye(rest)
    project = np.zeros((devices, HEIGHTS, 4 * TILE, width))
    merges = np.zeros((devices, 2, 3 * TILE, 3 * TILE))
    applies = np.zeros((devices, HEIGHTS, width, width + 4 * TILE))
    applies[..., :width] = matrix[:width, :width]
    for f, order in enumerate((list(range(devices)), list(range(devices))[::-1])):
        own, merge, apply = line_factors(matrix, devices, order)
        for z in range(HEIGHTS):
            spread = np.concatenate([place[z, z * TILE : (z + 1) * TILE], place[z, 2 * TILE :]], axis=0)
            project[:, z, 2 * f * TILE : 2 * (f + 1) * TILE] = spread @ own
            merges[:, f] += place[z] @ merge @ place[z].T
            applies[:, z, :, width + 2 * f * TILE : width + 2 * (f + 1) * TILE] = apply @ spread.T
    return project, merges, applies


def exchange_kernel(
    sizes, diff_ref, tur_ref, v_hbm, mx_hbm, wp_ref, wm_ref, wy_ref,
    v_scr, inflow_ref, rotor_ref,
    send_r, recv_r, send_l, recv_l, stage, mx_ref, masks, rot_acc, rot_send, rot_recv,
    mx_sem, load_sem, ssem_r, rsem_r, ssem_l, rsem_l, halo_ssem, halo_rsem, flow_ssem, flow_rsem,
    rot_ssem, rot_rsem,
):
    sections, devices, count, lead, hop = sizes
    zb = HEIGHTS
    _, depth, width, length = v_hbm.shape
    units = depth // zb
    turbines = tur_ref.shape[2]
    section, me, gz = lax.axis_index("sec"), lax.axis_index("gy"), lax.axis_index("gz")
    half = length // 2

    barrier = pltpu.get_barrier_semaphore()
    group = [(dy, dz) for dy in range(devices) for dz in range(count) if (dy, dz) != (0, 0)]
    peer = lambda dy, dz: {"gy": (me + dy) % devices, "gz": (gz + dz) % count}
    for dy, dz in group:
        pl.semaphore_signal(barrier, inc=1, device_id=peer(dy, dz), device_id_type=MESH)
    for ds in range(1, sections):
        pl.semaphore_signal(barrier, inc=1, device_id={"sec": (section + ds) % sections}, device_id_type=MESH)

    backward = (gz + count - 1) // count
    unit_of = lambda i: backward * (units - 1 - i) + (1 - backward) * i
    z_of = lambda i: unit_of(i) * zb

    def load(i):
        z0 = z_of(i)
        return pltpu.make_async_copy(v_hbm.at[:, pl.ds(z0, zb)], v_scr.at[:, pl.ds(z0 + 1, zb)], load_sem.at[i])

    @pl.loop(0, units)
    def _(i):
        load(i).start()

    matrices = pltpu.make_async_copy(mx_hbm, mx_ref, mx_sem)
    matrices.start()

    farm_row = (section + sections - 1) % sections % (sections - 1)
    corner = []
    for k in range(3):
        row = lax.broadcasted_iota(jnp.int32, (turbines, LANES), 0)
        got = jnp.zeros((turbines, LANES), jnp.int32)
        for t in range(turbines):
            got = jnp.where(row == t, tur_ref[farm_row, k, t], got)
        corner.append(got)
    ys = me * width + lax.broadcasted_iota(jnp.int32, (turbines, LANES), 1)
    spans = jnp.where((ys >= corner[1]) & (ys < corner[1] + DISK), 1.0, 0.0)
    masks[...] = jnp.concatenate([spans, jnp.zeros((16 - turbines, LANES), jnp.float32)], axis=0).astype(jnp.bfloat16)
    rot_acc[...] = jnp.zeros_like(rot_acc)

    flows = (
        (me, 1, send_r, recv_r, ssem_r, rsem_r),
        (devices - 1 - me, devices - 1, send_l, recv_l, ssem_l, rsem_l),
    )
    def message(f, i, c):
        _, step, sent, came, ssem, rsem = flows[f]
        return pltpu.make_async_remote_copy(
            sent.at[i, c], came.at[i, c], ssem.at[i, c], rsem.at[i, c],
            device_id={"gy": (me + step) % devices}, device_id_type=MESH,
        )

    def project(i):
        z0 = z_of(i)
        for c in range(3):
            rests = []
            for z in range(zb):
                wh, wl = wp_ref[me, z, 0], wp_ref[me, z, 1]
                high, low = split(v_scr[c, z0 + 1 + z])
                if c == 0:
                    tall = jnp.concatenate([wh, masks[:, :width]], axis=0)
                    got = mm(tall, high) + mm(tall, low)
                    zs = gz * depth + z0 + z
                    live = jnp.where((zs >= corner[2]) & (zs < corner[2] + DISK), 1.0, 0.0)
                    for q in range(length // LANES):
                        at = slice(q * LANES, (q + 1) * LANES)
                        rot_acc[:, at] += live * got[4 * TILE : 4 * TILE + turbines, at]
                    got = got[: 4 * TILE] + mm(wl, high)
                else:
                    got = mm(wh, high) + mm(wh, low) + mm(wl, high)
                send_r[i, c, z] = got[:TILE]
                send_l[i, c, z] = got[2 * TILE : 3 * TILE]
                rests.append((got[TILE : 2 * TILE], got[3 * TILE :]))
            send_r[i, c, 2] = rests[0][0] + rests[1][0]
            send_l[i, c, 2] = rests[0][1] + rests[1][1]

    def forward(f, q):
        place, _, sent, came, _, _ = flows[f]
        i, c = q // 3, q % 3

        @pl.when((q >= 0) & (q < 3 * units))
        def _():
            @pl.when(place > 0)
            def _():
                message(f, i, c).wait_recv()

            @pl.when((place > 0) & (place < devices - 1))
            def _():
                high, low = split(came[i, c].reshape(3 * TILE, length))
                wh, wl = wm_ref[me, f, 0], wm_ref[me, f, 1]
                got = mm(wh, high) + mm(wh, low) + mm(wl, high)
                sent[i, c] = sent[i, c] + got.reshape(3, TILE, length)

            @pl.when(place < devices - 1)
            def _():
                message(f, i, c).start()

    def relay(i, k):
        for f in range(2):
            forward(f, 3 * (i + lead) + k - hop * flows[f][0])

    def along(i):
        z0, slot = z_of(i), i % SLOTS
        rows = jnp.concatenate([v_scr[c, pl.ds(z0 + 1, zb)].reshape(zb * width, length) for c in range(3)], axis=0)
        wide = mx_ref.shape[-1]
        ahead = pltpu.roll(rows[:, length - wide :], wide - (half - (length - wide)), 1)
        sides = []
        for g, data in enumerate((rows[:, :wide] + ahead, rows[:, :wide] - ahead)):
            high, low = split(data)
            sides.append(mm(high, mx_ref[g, 0]) + mm(low, mx_ref[g, 0]) + mm(high, mx_ref[g, 1]))
        near, far = sides[0] + sides[1], sides[0] - sides[1]
        back = half % LANES
        far = pltpu.roll(far, back, 1)
        cut = half - back
        lane = lax.broadcasted_iota(jnp.int32, (rows.shape[0], LANES), 1)
        seam = jnp.where(lane < back, near[:, cut : cut + LANES], far[:, :LANES])
        slope = jnp.concatenate([near[:, :cut], seam, far[:, LANES : LANES + length - cut - LANES]], axis=1)
        for c in range(3):
            for z in range(zb):
                here = v_scr[c, z0 + 1 + z]
                at = (c * zb + z) * width
                laplace = v_scr[c, z0 + z] + v_scr[c, z0 + 2 + z] - 2.0 * here
                tendency = (1.0 + v_scr[0, z0 + 1 + z]) * slope[at : at + width]
                stage[slot, c, z] = here - time_step * tendency + diff_ref[z0 + z] * laplace

    def across(i):
        z0, slot = z_of(i), i % SLOTS
        for z in range(zb):
            wh, wl = wy_ref[me, z, 0], wy_ref[me, z, 1]
            speed = v_scr[1, z0 + 1 + z]
            for c in range(3):
                parts = [v_scr[c, z0 + 1 + z], recv_r[i, c, z], recv_r[i, c, 2], recv_l[i, c, z], recv_l[i, c, 2]]
                high, low = split(jnp.concatenate(parts, axis=0))
                slope = mm(wh, high) + mm(wh, low) + mm(wl, high)
                v_scr[c, z0 + 1 + z] = stage[slot, c, z] - time_step * (speed * slope)

    up = lambda: pltpu.make_async_remote_copy(
        v_hbm.at[:, depth - 1], v_scr.at[:, 0], halo_ssem.at[0], halo_rsem.at[0],
        device_id={"gz": (gz + 1) % count}, device_id_type=MESH,
    )
    down = lambda: pltpu.make_async_remote_copy(
        v_hbm.at[:, 0], v_scr.at[:, depth + 1], halo_ssem.at[1], halo_rsem.at[1],
        device_id={"gz": (gz + count - 1) % count}, device_id_type=MESH,
    )

    lanes = pl.ds(length - FRINGE, FRINGE)

    def flow(i, to):
        z0 = z_of(i)
        return pltpu.make_async_remote_copy(
            v_scr.at[:, pl.ds(z0 + 1, zb), :, lanes], inflow_ref.at[:, pl.ds(z0, zb)], flow_ssem.at[to - 1, i], flow_rsem.at[i],
            device_id={"sec": to}, device_id_type=MESH,
        )

    def pass_on(i):
        z0 = z_of(i)
        here = inflow_ref.at[:, pl.ds(z0, zb)]
        return pltpu.make_async_remote_copy(
            here, here, flow_ssem.at[0, i], flow_rsem.at[i], device_id={"sec": (section + 1) % sections}, device_id_type=MESH
        )

    direct = [to for to in (1, 2) if to < sections]

    def emit(i):
        @pl.when(section == 0)
        def _():
            for to in direct[::-1]:
                flow(i, to).start()

    def take(i):
        @pl.when(section > 0)
        def _():
            pass_on(i).wait_recv()

        @pl.when((section > 1) & (section < sections - 1))
        def _():
            pass_on(i).start()

    def wait_halo(i):
        @pl.when((unit_of(i) == 0) & (gz > 0))
        def _():
            up().wait_recv()

        @pl.when((unit_of(i) == units - 1) & (gz < count - 1))
        def _():
            down().wait_recv()

    def step(i, with_project, with_along, with_across):
        if with_project:

            @pl.when(section != 1)
            def _():
                load(i + lead).wait()
                if not with_along:
                    project(i + lead)

        if with_along:
            wait_halo(i)
        if with_project and with_along:
            project(i + lead)
        if with_project or with_along:
            relay(i, 0)
        if with_along:
            along(i)
        if with_along and not with_project:
            rotor_sums(i)
        if with_project or with_along:
            relay(i, 1)
        if with_across:
            across(i - LAG)
            emit(i - LAG)

            @pl.when(i >= LAG + 2)
            def _():
                take(i - LAG - 2)

        if with_project or with_along:
            relay(i, 2)

    def run(low, high, *flags):
        if high > low:

            @pl.loop(low, high)
            def _(i):
                step(i, *flags)

    rotor = lambda at: pltpu.make_async_remote_copy(
        rot_send, rot_recv.at[at], rot_ssem.at[at], rot_rsem.at[at], device_id=peer(*group[at]), device_id_type=MESH
    )

    def rotor_sums(i):
        @pl.when(i == units - lead)
        def _():
            xs = lax.broadcasted_iota(jnp.int32, (turbines, LANES), 1)
            folded = jnp.zeros((turbines, LANES), jnp.float32)
            for q in range(length // LANES):
                folded = folded + jnp.where(xs + q * LANES == corner[0], rot_acc[:, q * LANES : (q + 1) * LANES], 0.0)
            rot_send[...] = folded

        @pl.when(i == units - lead + 1)
        def _():
            for at in range(len(group)):
                rotor(at).start()

    @pl.when(section == 1)
    def _():
        @pl.loop(0, units)
        def _(i):
            load(i).wait()

        @pl.loop(1, lead)
        def _(i):
            project(i)

    @pl.when(section != 1)
    def _():
        load(0).wait()

    project(0)
    pl.semaphore_wait(barrier, len(group) + sections - 1)
    for k in range(3):
        relay(-lead, k)

    @pl.when(gz < count - 1)
    def _():
        up().start()

    @pl.when(gz > 0)
    def _():
        down().start()

    run(-lead + 1, 0, True, False, False)
    @pl.when(gz == 0)
    def _():
        v_scr[:, 0] = jnp.zeros((3, width, length), jnp.float32)

    @pl.when(gz == count - 1)
    def _():
        v_scr[:, depth + 1] = jnp.zeros((3, width, length), jnp.float32)

    for place, _, _, came, _, _ in flows:

        @pl.when(place == 0)
        def _():
            @pl.loop(0, units)
            def _(i):
                came[i] = jnp.zeros(came.shape[1:], jnp.float32)

    matrices.wait()
    run(0, LAG, True, True, False)
    run(LAG, units - lead, True, True, True)
    run(units - lead, units, False, True, True)
    run(units, units + LAG, False, False, True)

    total = rot_send[...]
    for at in range(len(group)):
        rotor(at).wait()
        total = total + rot_recv[at]
    rotor_ref[...] = total

    @pl.when(gz < count - 1)
    def _():
        up().wait_send()

    @pl.when(gz > 0)
    def _():
        down().wait_send()

    for f in range(2):

        @pl.when(flows[f][0] < devices - 1)
        def _():
            @pl.loop(0, units)
            def _(i):
                for c in range(3):
                    message(f, i, c).wait_send()

    @pl.when(section == 0)
    def _():
        @pl.loop(0, units)
        def _(i):
            for to in direct:
                flow(i, to).wait_send()

    @pl.loop(units - 2, units)
    def _(i):
        take(i)

    @pl.when((section > 1) & (section < sections - 1))
    def _():
        @pl.loop(0, units)
        def _(i):
            pass_on(i).wait_send()


def finish_kernel(sections, tur_ref, start_ref, adv_ref, inflow_ref, rotor_ref, out_ref, weights, pushes):
    section, me, gz = lax.axis_index("sec"), lax.axis_index("gy"), lax.axis_index("gz")
    _, zb, width, length = out_ref.shape
    base = pl.program_id(0) * zb
    farm = (section + sections - 1) % sections % (sections - 1)
    out_ref[...] = adv_ref[:, pl.ds(base + 1, zb)]

    @pl.when(section > 0)
    def _():
        y0, z0 = me * width, (gz * pl.num_programs(0) + pl.program_id(0)) * zb
        start = start_ref[farm]
        turn = lax.rem(start, LANES)

        @pl.when(pl.program_id(0) == 0)
        def _():
            speed = 1.0 + jnp.sum(rotor_ref[...], axis=1, keepdims=True) / (DISK * DISK)
            thrust = -0.5 * thrust_coef * speed * jnp.abs(speed)
            pushes[...] = jnp.broadcast_to(time_step * thrust, pushes.shape)
            offset = lax.broadcasted_iota(jnp.int32, weights.shape, 0) // 8 * LANES - turn
            offset = offset + lax.broadcasted_iota(jnp.int32, weights.shape, 1)
            inside = (offset >= 0) & (offset < FRINGE)
            weights[...] = jnp.where(inside, jnp.sin(jnp.pi * (offset.astype(jnp.float32) + 0.5) / FRINGE) ** 2, 0.0)

        for t in range(tur_ref.shape[2]):
            tx, ty, tz = (tur_ref[farm, k, t] for k in range(3))

            @pl.when((tz < z0 + zb) & (tz + DISK > z0) & (ty < y0 + width) & (ty + DISK > y0))
            def _():
                shape = (zb, width, LANES)
                zs = z0 + lax.broadcasted_iota(jnp.int32, shape, 0)
                ys = y0 + lax.broadcasted_iota(jnp.int32, shape, 1)
                left = pl.multiple_of(tx // LANES * LANES, LANES)
                xs = left + lax.broadcasted_iota(jnp.int32, shape, 2)
                hit = (xs == tx) & (ys >= ty) & (ys < ty + DISK) & (zs >= tz) & (zs < tz + DISK)
                push = pushes[t : t + 1].reshape(1, 1, LANES)
                at = pl.ds(left, LANES)
                out_ref[0, :, :, at] = out_ref[0, :, :, at] + jnp.where(hit, push, 0.0)

        for j in range(2):

            @pl.when(start // LANES + j < length // LANES)
            def _():
                left = pl.multiple_of((start // LANES + j) * LANES, LANES)
                at = pl.ds(left, LANES)
                weight = weights[8 * j : 8 * j + 1]
                for c in range(3):
                    for z in range(zb):
                        here = out_ref[c, z, :, at]
                        out_ref[c, z, :, at] = here + weight * (pltpu.roll(inflow_ref[c, base + z], turn, 1) - here)


def cost(flops, bytes_accessed):
    return pl.CostEstimate(flops=int(flops), bytes_accessed=int(bytes_accessed), transcendentals=0)


def body(velocity, diffusion, turbines, fringe_start):
    current = velocity[0]
    _, depth, width, length = current.shape
    sections, devices, count = (lax.axis_size(a) for a in ("sec", "gy", "gz"))
    f32, bf16 = jnp.float32, jnp.bfloat16
    units = depth // HEIGHTS
    hop = max(1, 12 // (devices - 1))
    lead = -(-hop * (devices - 1) // 3)
    rows = 3 * depth
    half = length // 2
    wide = -(-half // LANES) * LANES
    number = turbines.shape[1]
    turbines = jnp.swapaxes(turbines, 1, 2)

    straight = slope_matrix(length)
    mx = np.zeros((2, wide, wide))
    mx[0, :half, :half] = 0.5 * (straight[:half, :half] + straight[:half, half:]).T
    mx[1, :half, :half] = 0.5 * (straight[:half, :half] - straight[:half, half:]).T
    factors = flow_factors(slope_matrix(width * devices), devices)
    pair = lambda x: np.moveaxis(halves(x), 0, -3)
    consts = [jnp.asarray(pair(x)) for x in (mx, *factors)]

    vmem = pl.BlockSpec(memory_space=pltpu.VMEM)
    smem = pl.BlockSpec(memory_space=pltpu.SMEM)
    hbm = pl.BlockSpec(memory_space=pl.ANY)
    message = pltpu.VMEM((units, 3, 3, TILE, length), f32)
    dma = pltpu.SemaphoreType.DMA
    others = devices * count - 1
    advanced, inflow, rotor = pl.pallas_call(
        functools.partial(exchange_kernel, (sections, devices, count, lead, hop)),
        out_shape=(
            pltpu.VMEM((3, depth + 2, width, length), f32),
            pltpu.VMEM((3, depth, width, FRINGE), f32),
            pltpu.VMEM((number, LANES), f32),
        ),
        in_specs=[smem, smem, hbm, hbm, vmem, vmem, vmem],
        out_specs=(vmem, vmem, vmem),
        scratch_shapes=[
            message, message, message, message,
            pltpu.VMEM((SLOTS, 3, HEIGHTS, width, length), f32),
            pltpu.VMEM(consts[0].shape, bf16),
            pltpu.VMEM((16, LANES), bf16),
            pltpu.VMEM((number, length), f32),
            pltpu.VMEM((number, LANES), f32),
            pltpu.VMEM((others, number, LANES), f32),
            dma, dma((units,)), dma((units, 3)), dma((units, 3)), dma((units, 3)), dma((units, 3)), dma((2,)), dma((2,)),
            dma((2, units)), dma((units,)), dma((others,)), dma((others,)),
        ],
        compiler_params=pltpu.CompilerParams(collective_id=0, has_side_effects=True, vmem_limit_bytes=30 * 1024 * 1024),
        cost_estimate=cost(6 * rows * width * length * length, 12 * rows * width * length),
        name="exchange",
    )(diffusion, turbines, current, *consts)

    zc = min(8, depth)
    out = pl.pallas_call(
        functools.partial(finish_kernel, sections),
        out_shape=jax.ShapeDtypeStruct(current.shape, f32),
        grid_spec=pltpu.PrefetchScalarGridSpec(
            num_scalar_prefetch=2,
            grid=(depth // zc,),
            in_specs=[
                vmem, vmem, vmem,
            ],
            out_specs=pl.BlockSpec((3, zc, width, length), lambda i, *_: (0, i, 0, 0)),
            scratch_shapes=[pltpu.VMEM((16, LANES), f32), pltpu.VMEM((number, LANES), f32)],
        ),
        compiler_params=pltpu.CompilerParams(dimension_semantics=("arbitrary",), vmem_limit_bytes=30 * 1024 * 1024),
        cost_estimate=cost(rows * width * length, 8 * rows * width * length),
        name="finish",
    )(turbines, fringe_start, *(pltpu.with_memory_space_constraint(x, pltpu.VMEM) for x in (advanced, inflow, rotor)))
    return out[None]


def solution(mesh):
    in_specs = (P("sec", None, "gz", "gy", None), P("gz"), P(), P())
    out_specs = P("sec", None, "gz", "gy", None)
    return jax.shard_map(body, mesh=mesh, in_specs=in_specs, out_specs=out_specs, check_vma=False)
```

```python
import functools

import jax
import jax.numpy as jnp
import numpy as np
from jax import lax
from jax.experimental import pallas as pl
from jax.experimental.pallas import tpu as pltpu
from jax.sharding import PartitionSpec as P

FRINGE = 128
DISK = 16
LANES = 128
RANK = 12
TILE = 8
HEIGHTS = 2
LAG = 1
SLOTS = 2

time_step = 0.2
thrust_coef = 1.5

MESH = pl.DeviceIdType.MESH


def slope_matrix(n):
    i = np.arange(n)
    d = (i[:, None] - i[None, :]) % n
    safe = np.where(d == 0, 1, d)
    return np.where(d == 0, 0.0, np.pi / n * (1.0 - 2.0 * (d % 2)) / np.tan(safe * np.pi / n))


def leading(matrix, keep):
    basis = np.linalg.svd(matrix)[2][:keep].T
    signs = np.sign(basis[np.argmax(np.abs(basis), axis=0), np.arange(basis.shape[1])])
    return np.round(basis * signs * 2.0**25) / 2.0**25


def halves(x):
    x = np.asarray(x, np.float32)
    high = x.astype(jnp.bfloat16)
    return np.stack([high, (x - high.astype(np.float32)).astype(jnp.bfloat16)])


def split(x):
    high = x.astype(jnp.bfloat16)
    return high, (x - high.astype(jnp.float32)).astype(jnp.bfloat16)


def mm(a, b):
    return jnp.dot(a, b, preferred_element_type=jnp.float32)


def line_factors(matrix, devices, order):
    width = matrix.shape[0] // devices
    block = lambda a, b: matrix[a * width : (a + 1) * width, b * width : (b + 1) * width]
    own = np.zeros((devices, RANK, width))
    merge = np.zeros((devices, RANK, RANK))
    apply = np.zeros((devices, width, RANK))
    before = None
    for at, here in enumerate(order):
        if before is not None:
            apply[here] = before[:width]
            before = before[width:]
        ahead = order[at + 1 :]
        if not ahead:
            continue
        rows = np.concatenate([np.concatenate([block(a, b) for b in order[: at + 1]], axis=1) for a in ahead], axis=0)
        held = leading(rows.T, RANK)
        own[here] = held.T @ rows[:, at * width :]
        if before is not None:
            merge[here] = held.T @ before
        before = held
    return own, merge, apply


def flow_factors(matrix, devices):
    width = matrix.shape[0] // devices
    rest = RANK - TILE
    place = np.zeros((HEIGHTS, 3 * TILE, RANK))
    for z in range(HEIGHTS):
        place[z, z * TILE : (z + 1) * TILE, :TILE] = np.eye(TILE)
        place[z, 2 * TILE + z * rest : 2 * TILE + (z + 1) * rest, TILE:] = np.eye(rest)
    project = np.zeros((devices, HEIGHTS, 4 * TILE, width))
    merges = np.zeros((devices, 2, 3 * TILE, 3 * TILE))
    applies = np.zeros((devices, HEIGHTS, width, width + 4 * TILE))
    applies[..., :width] = matrix[:width, :width]
    for f, order in enumerate((list(range(devices)), list(range(devices))[::-1])):
        own, merge, apply = line_factors(matrix, devices, order)
        for z in range(HEIGHTS):
            spread = np.concatenate([place[z, z * TILE : (z + 1) * TILE], place[z, 2 * TILE :]], axis=0)
            project[:, z, 2 * f * TILE : 2 * (f + 1) * TILE] = spread @ own
            merges[:, f] += place[z] @ merge @ place[z].T
            applies[:, z, :, width + 2 * f * TILE : width + 2 * (f + 1) * TILE] = apply @ spread.T
    return project, merges, applies


def exchange_kernel(
    sizes, diff_ref, tur_ref, v_hbm, mx_hbm, wp_ref, wm_ref, wy_ref,
    v_scr, inflow_ref, rotor_ref,
    send_r, recv_r, send_l, recv_l, stage, mx_ref, masks, rot_acc, rot_send, rot_recv,
    mx_sem, load_sem, ssem_r, rsem_r, ssem_l, rsem_l, halo_ssem, halo_rsem, flow_ssem, flow_rsem,
    rot_ssem, rot_rsem,
):
    sections, devices, count, lead, hop = sizes
    zb = HEIGHTS
    _, depth, width, length = v_hbm.shape
    units = depth // zb
    turbines = tur_ref.shape[2]
    section, me, gz = lax.axis_index("sec"), lax.axis_index("gy"), lax.axis_index("gz")
    half = length // 2

    barrier = pltpu.get_barrier_semaphore()
    group = [(dy, dz) for dy in range(devices) for dz in range(count) if (dy, dz) != (0, 0)]
    peer = lambda dy, dz: {"gy": (me + dy) % devices, "gz": (gz + dz) % count}
    for dy, dz in group:
        pl.semaphore_signal(barrier, inc=1, device_id=peer(dy, dz), device_id_type=MESH)
    for ds in range(1, sections):
        pl.semaphore_signal(barrier, inc=1, device_id={"sec": (section + ds) % sections}, device_id_type=MESH)

    backward = (gz + count - 1) // count
    unit_of = lambda i: backward * (units - 1 - i) + (1 - backward) * i
    z_of = lambda i: unit_of(i) * zb

    def load(i):
        z0 = z_of(i)
        return pltpu.make_async_copy(v_hbm.at[:, pl.ds(z0, zb)], v_scr.at[:, pl.ds(z0 + 1, zb)], load_sem.at[i])

    @pl.loop(0, units)
    def _(i):
        load(i).start()

    matrices = pltpu.make_async_copy(mx_hbm, mx_ref, mx_sem)
    matrices.start()

    farm_row = (section + sections - 1) % sections % (sections - 1)
    corner = []
    for k in range(3):
        row = lax.broadcasted_iota(jnp.int32, (turbines, LANES), 0)
        got = jnp.zeros((turbines, LANES), jnp.int32)
        for t in range(turbines):
            got = jnp.where(row == t, tur_ref[farm_row, k, t], got)
        corner.append(got)
    ys = me * width + lax.broadcasted_iota(jnp.int32, (turbines, LANES), 1)
    spans = jnp.where((ys >= corner[1]) & (ys < corner[1] + DISK), 1.0, 0.0)
    masks[...] = jnp.concatenate([spans, jnp.zeros((16 - turbines, LANES), jnp.float32)], axis=0).astype(jnp.bfloat16)
    rot_acc[...] = jnp.zeros_like(rot_acc)

    flows = (
        (me, 1, send_r, recv_r, ssem_r, rsem_r),
        (devices - 1 - me, devices - 1, send_l, recv_l, ssem_l, rsem_l),
    )
    def message(f, i, c):
        _, step, sent, came, ssem, rsem = flows[f]
        return pltpu.make_async_remote_copy(
            sent.at[i, c], came.at[i, c], ssem.at[i, c], rsem.at[i, c],
            device_id={"gy": (me + step) % devices}, device_id_type=MESH,
        )

    def project(i):
        z0 = z_of(i)
        for c in range(3):
            rests = []
            for z in range(zb):
                wh, wl = wp_ref[me, z, 0], wp_ref[me, z, 1]
                high, low = split(v_scr[c, z0 + 1 + z])
                if c == 0:
                    tall = jnp.concatenate([wh, masks[:, :width]], axis=0)
                    got = mm(tall, high) + mm(tall, low)
                    zs = gz * depth + z0 + z
                    live = jnp.where((zs >= corner[2]) & (zs < corner[2] + DISK), 1.0, 0.0)
                    for q in range(length // LANES):
                        at = slice(q * LANES, (q + 1) * LANES)
                        rot_acc[:, at] += live * got[4 * TILE : 4 * TILE + turbines, at]
                    got = got[: 4 * TILE] + mm(wl, high)
                else:
                    got = mm(wh, high) + mm(wh, low) + mm(wl, high)
                send_r[i, c, z] = got[:TILE]
                send_l[i, c, z] = got[2 * TILE : 3 * TILE]
                rests.append((got[TILE : 2 * TILE], got[3 * TILE :]))
            send_r[i, c, 2] = rests[0][0] + rests[1][0]
            send_l[i, c, 2] = rests[0][1] + rests[1][1]

    def forward(f, q):
        place, _, sent, came, _, _ = flows[f]
        i, c = q // 3, q % 3

        @pl.when((q >= 0) & (q < 3 * units))
        def _():
            @pl.when(place > 0)
            def _():
                message(f, i, c).wait_recv()

            @pl.when((place > 0) & (place < devices - 1))
            def _():
                high, low = split(came[i, c].reshape(3 * TILE, length))
                wh, wl = wm_ref[me, f, 0], wm_ref[me, f, 1]
                got = mm(wh, high) + mm(wh, low) + mm(wl, high)
                sent[i, c] = sent[i, c] + got.reshape(3, TILE, length)

            @pl.when(place < devices - 1)
            def _():
                message(f, i, c).start()

    def relay(i, k):
        for f in range(2):
            forward(f, 3 * (i + lead) + k - hop * flows[f][0])

    def along(i):
        z0, slot = z_of(i), i % SLOTS
        rows = jnp.concatenate([v_scr[c, pl.ds(z0 + 1, zb)].reshape(zb * width, length) for c in range(3)], axis=0)
        wide = mx_ref.shape[-1]
        ahead = pltpu.roll(rows[:, length - wide :], wide - (half - (length - wide)), 1)
        sides = []
        for g, data in enumerate((rows[:, :wide] + ahead, rows[:, :wide] - ahead)):
            high, low = split(data)
            sides.append(mm(high, mx_ref[g, 0]) + mm(low, mx_ref[g, 0]) + mm(high, mx_ref[g, 1]))
        near, far = sides[0] + sides[1], sides[0] - sides[1]
        back = half % LANES
        far = pltpu.roll(far, back, 1)
        cut = half - back
        lane = lax.broadcasted_iota(jnp.int32, (rows.shape[0], LANES), 1)
        seam = jnp.where(lane < back, near[:, cut : cut + LANES], far[:, :LANES])
        slope = jnp.concatenate([near[:, :cut], seam, far[:, LANES : LANES + length - cut - LANES]], axis=1)
        for c in range(3):
            for z in range(zb):
                here = v_scr[c, z0 + 1 + z]
                at = (c * zb + z) * width
                laplace = v_scr[c, z0 + z] + v_scr[c, z0 + 2 + z] - 2.0 * here
                tendency = (1.0 + v_scr[0, z0 + 1 + z]) * slope[at : at + width]
                stage[slot, c, z] = here - time_step * tendency + diff_ref[z0 + z] * laplace

    def across(i):
        z0, slot = z_of(i), i % SLOTS
        for z in range(zb):
            wh, wl = wy_ref[me, z, 0], wy_ref[me, z, 1]
            speed = v_scr[1, z0 + 1 + z]
            for c in range(3):
                parts = [v_scr[c, z0 + 1 + z], recv_r[i, c, z], recv_r[i, c, 2], recv_l[i, c, z], recv_l[i, c, 2]]
                high, low = split(jnp.concatenate(parts, axis=0))
                slope = mm(wh, high) + mm(wh, low) + mm(wl, high)
                v_scr[c, z0 + 1 + z] = stage[slot, c, z] - time_step * (speed * slope)

    up = lambda: pltpu.make_async_remote_copy(
        v_hbm.at[:, depth - 1], v_scr.at[:, 0], halo_ssem.at[0], halo_rsem.at[0],
        device_id={"gz": (gz + 1) % count}, device_id_type=MESH,
    )
    down = lambda: pltpu.make_async_remote_copy(
        v_hbm.at[:, 0], v_scr.at[:, depth + 1], halo_ssem.at[1], halo_rsem.at[1],
        device_id={"gz": (gz + count - 1) % count}, device_id_type=MESH,
    )

    lanes = pl.ds(length - FRINGE, FRINGE)

    def flow(i, to):
        z0 = z_of(i)
        return pltpu.make_async_remote_copy(
            v_scr.at[:, pl.ds(z0 + 1, zb), :, lanes], inflow_ref.at[:, pl.ds(z0, zb)], flow_ssem.at[to - 1, i], flow_rsem.at[i],
            device_id={"sec": to}, device_id_type=MESH,
        )

    def pass_on(i):
        z0 = z_of(i)
        here = inflow_ref.at[:, pl.ds(z0, zb)]
        return pltpu.make_async_remote_copy(
            here, here, flow_ssem.at[0, i], flow_rsem.at[i], device_id={"sec": (section + 1) % sections}, device_id_type=MESH
        )

    direct = [to for to in (1, 2) if to < sections]

    def emit(i):
        @pl.when(section == 0)
        def _():
            for to in direct[::-1]:
                flow(i, to).start()

    def take(i):
        @pl.when(section > 0)
        def _():
            pass_on(i).wait_recv()

        @pl.when((section > 1) & (section < sections - 1))
        def _():
            pass_on(i).start()

    def wait_halo(i):
        @pl.when((unit_of(i) == 0) & (gz > 0))
        def _():
            up().wait_recv()

        @pl.when((unit_of(i) == units - 1) & (gz < count - 1))
        def _():
            down().wait_recv()

    def rotor_sums(i):
        @pl.when(i == units - lead)
        def _():
            xs = lax.broadcasted_iota(jnp.int32, (turbines, LANES), 1)
            folded = jnp.zeros((turbines, LANES), jnp.float32)
            for q in range(length // LANES):
                folded = folded + jnp.where(xs + q * LANES == corner[0], rot_acc[:, q * LANES : (q + 1) * LANES], 0.0)
            rot_send[...] = folded

        @pl.when(i == units - lead + 1)
        def _():
            for at in range(len(group)):
                rotor(at).start()

    def finish(i):
        across(i)
        emit(i)

        @pl.when(i >= 2)
        def _():
            take(i - 2)

    rotor = lambda at: pltpu.make_async_remote_copy(
        rot_send, rot_recv.at[at], rot_ssem.at[at], rot_rsem.at[at], device_id=peer(*group[at]), device_id_type=MESH
    )

    @pl.when(section == 1)
    def _():
        @pl.loop(0, units)
        def _(i):
            load(i).wait()

        @pl.loop(1, lead)
        def _(i):
            project(i)

    @pl.when(section != 1)
    def _():
        load(0).wait()

    project(0)
    pl.semaphore_wait(barrier, len(group) + sections - 1)
    for k in range(3):
        relay(-lead, k)

    @pl.when(gz < count - 1)
    def _():
        up().start()

    @pl.when(gz > 0)
    def _():
        down().start()

    @pl.loop(-lead + 1, 0)
    def _(i):
        @pl.when(section != 1)
        def _():
            load(i + lead).wait()
            project(i + lead)

        for k in range(3):
            relay(i, k)

    @pl.when(gz == 0)
    def _():
        v_scr[:, 0] = jnp.zeros((3, width, length), jnp.float32)

    @pl.when(gz == count - 1)
    def _():
        v_scr[:, depth + 1] = jnp.zeros((3, width, length), jnp.float32)

    for place, _, _, came, _, _ in flows:

        @pl.when(place == 0)
        def _():
            @pl.loop(0, units)
            def _(i):
                came[i] = jnp.zeros(came.shape[1:], jnp.float32)

    matrices.wait()
    @pl.loop(0, units)
    def _(i):
        wait_halo(i)

        @pl.when(i < units - lead)
        def _():
            @pl.when(section != 1)
            def _():
                load(i + lead).wait()

            project(i + lead)

        relay(i, 0)
        along(i)
        rotor_sums(i)
        relay(i, 1)

        @pl.when(i >= LAG)
        def _():
            finish(i - LAG)

        relay(i, 2)

    @pl.loop(units - LAG, units)
    def _(i):
        finish(i)

    total = rot_send[...]
    for at in range(len(group)):
        rotor(at).wait()
        total = total + rot_recv[at]
    rotor_ref[...] = total

    @pl.when(gz < count - 1)
    def _():
        up().wait_send()

    @pl.when(gz > 0)
    def _():
        down().wait_send()

    for f in range(2):

        @pl.when(flows[f][0] < devices - 1)
        def _():
            @pl.loop(0, units)
            def _(i):
                for c in range(3):
                    message(f, i, c).wait_send()

    @pl.when(section == 0)
    def _():
        @pl.loop(0, units)
        def _(i):
            for to in direct:
                flow(i, to).wait_send()

    @pl.loop(units - 2, units)
    def _(i):
        take(i)

    @pl.when((section > 1) & (section < sections - 1))
    def _():
        @pl.loop(0, units)
        def _(i):
            pass_on(i).wait_send()


def finish_kernel(sections, tur_ref, start_ref, _, inflow_ref, rotor_ref, out_hbm, v_ref, sems):
    section, me, gz = lax.axis_index("sec"), lax.axis_index("gy"), lax.axis_index("gz")
    _, depth, width, length = out_hbm.shape
    zb = depth // sems.shape[0]
    farm = (section + sections - 1) % sections % (sections - 1)

    def store(i):
        z0 = i * zb
        return pltpu.make_async_copy(v_ref.at[:, pl.ds(z0 + 1, zb)], out_hbm.at[:, pl.ds(z0, zb)], sems.at[i])

    @pl.when(section == 0)
    def _():
        @pl.loop(0, depth // zb)
        def _(i):
            store(i).start()

    @pl.when(section > 0)
    def _():
        speed = 1.0 + jnp.sum(rotor_ref[...], axis=1, keepdims=True) / (DISK * DISK)
        push = jnp.broadcast_to(time_step * (-0.5 * thrust_coef * speed * jnp.abs(speed)), rotor_ref.shape)
        start = start_ref[farm]
        turn = lax.rem(start, LANES)
        offset = lax.broadcasted_iota(jnp.int32, (16, LANES), 0) // 8 * LANES - turn
        offset = offset + lax.broadcasted_iota(jnp.int32, (16, LANES), 1)
        inside = (offset >= 0) & (offset < FRINGE)
        weights = jnp.where(inside, jnp.sin(jnp.pi * (offset.astype(jnp.float32) + 0.5) / FRINGE) ** 2, 0.0)

        @pl.loop(0, depth // zb)
        def _(i):
            y0, here0 = me * width, i * zb
            z0 = gz * depth + here0
            for t in range(tur_ref.shape[2]):
                tx, ty, tz = (tur_ref[farm, k, t] for k in range(3))

                @pl.when((tz < z0 + zb) & (tz + DISK > z0) & (ty < y0 + width) & (ty + DISK > y0))
                def _():
                    at = pl.ds(pl.multiple_of(tx // LANES * LANES, LANES), LANES)
                    shape = (width, LANES)
                    ys = y0 + lax.broadcasted_iota(jnp.int32, shape, 0)
                    xs = tx // LANES * LANES + lax.broadcasted_iota(jnp.int32, shape, 1)
                    disk = (xs == tx) & (ys >= ty) & (ys < ty + DISK)
                    for z in range(zb):
                        hit = disk & (z0 + z >= tz) & (z0 + z < tz + DISK)
                        v_ref[0, here0 + z + 1, :, at] = v_ref[0, here0 + z + 1, :, at] + jnp.where(hit, push[t : t + 1], 0.0)

            for j in range(2):

                @pl.when(start // LANES + j < length // LANES)
                def _():
                    at = pl.ds(pl.multiple_of((start // LANES + j) * LANES, LANES), LANES)
                    weight = weights[8 * j : 8 * j + 1]
                    for c in range(3):
                        for z in range(zb):
                            here = v_ref[c, here0 + z + 1, :, at]
                            flown = pltpu.roll(inflow_ref[c, here0 + z], turn, 1)
                            v_ref[c, here0 + z + 1, :, at] = here + weight * (flown - here)

            store(i).start()

    @pl.loop(0, depth // zb)
    def _(i):
        store(i).wait()


def cost(flops, bytes_accessed):
    return pl.CostEstimate(flops=int(flops), bytes_accessed=int(bytes_accessed), transcendentals=0)


def body(velocity, diffusion, turbines, fringe_start):
    current = velocity[0]
    _, depth, width, length = current.shape
    sections, devices, count = (lax.axis_size(a) for a in ("sec", "gy", "gz"))
    f32, bf16 = jnp.float32, jnp.bfloat16
    units = depth // HEIGHTS
    hop = max(1, 12 // (devices - 1))
    lead = -(-hop * (devices - 1) // 3)
    rows = 3 * depth
    half = length // 2
    wide = -(-half // LANES) * LANES
    number = turbines.shape[1]
    turbines = jnp.swapaxes(turbines, 1, 2)

    straight = slope_matrix(length)
    mx = np.zeros((2, wide, wide))
    mx[0, :half, :half] = 0.5 * (straight[:half, :half] + straight[:half, half:]).T
    mx[1, :half, :half] = 0.5 * (straight[:half, :half] - straight[:half, half:]).T
    factors = flow_factors(slope_matrix(width * devices), devices)
    pair = lambda x: np.moveaxis(halves(x), 0, -3)
    consts = [jnp.asarray(pair(x)) for x in (mx, *factors)]

    vmem = pl.BlockSpec(memory_space=pltpu.VMEM)
    smem = pl.BlockSpec(memory_space=pltpu.SMEM)
    hbm = pl.BlockSpec(memory_space=pl.ANY)
    message = pltpu.VMEM((units, 3, 3, TILE, length), f32)
    dma = pltpu.SemaphoreType.DMA
    others = devices * count - 1
    advanced, inflow, rotor = pl.pallas_call(
        functools.partial(exchange_kernel, (sections, devices, count, lead, hop)),
        out_shape=(
            pltpu.VMEM((3, depth + 2, width, length), f32),
            pltpu.VMEM((3, depth, width, FRINGE), f32),
            pltpu.VMEM((number, LANES), f32),
        ),
        in_specs=[smem, smem, hbm, hbm, vmem, vmem, vmem],
        out_specs=(vmem, vmem, vmem),
        scratch_shapes=[
            message, message, message, message,
            pltpu.VMEM((SLOTS, 3, HEIGHTS, width, length), f32),
            pltpu.VMEM(consts[0].shape, bf16),
            pltpu.VMEM((16, LANES), bf16),
            pltpu.VMEM((number, length), f32),
            pltpu.VMEM((number, LANES), f32),
            pltpu.VMEM((others, number, LANES), f32),
            dma, dma((units,)), dma((units, 3)), dma((units, 3)), dma((units, 3)), dma((units, 3)), dma((2,)), dma((2,)),
            dma((2, units)), dma((units,)), dma((others,)), dma((others,)),
        ],
        compiler_params=pltpu.CompilerParams(collective_id=0, has_side_effects=True, vmem_limit_bytes=30 * 1024 * 1024),
        cost_estimate=cost(6 * rows * width * length * length, 12 * rows * width * length),
        name="exchange",
    )(diffusion, turbines, current, *consts)

    chip = lambda x: pltpu.with_memory_space_constraint(x, pltpu.VMEM)
    out, _ = pl.pallas_call(
        functools.partial(finish_kernel, sections),
        out_shape=(jax.ShapeDtypeStruct(current.shape, f32), pltpu.VMEM((3, depth + 2, width, length), f32)),
        in_specs=[smem, smem, vmem, vmem, vmem],
        out_specs=(hbm, vmem),
        scratch_shapes=[dma((depth // min(4, depth),))],
        input_output_aliases={2: 1},
        compiler_params=pltpu.CompilerParams(vmem_limit_bytes=30 * 1024 * 1024),
        cost_estimate=cost(rows * width * length, 8 * rows * width * length),
        name="finish",
    )(turbines, fringe_start, chip(advanced), chip(inflow), chip(rotor))
    return out[None]


def solution(mesh):
    in_specs = (P("sec", None, "gz", "gy", None), P("gz"), P(), P())
    out_specs = P("sec", None, "gz", "gy", None)
    return jax.shard_map(body, mesh=mesh, in_specs=in_specs, out_specs=out_specs, check_vma=False)
```

```python
import functools

import jax
import jax.numpy as jnp
import numpy as np
from jax import lax
from jax.experimental import pallas as pl
from jax.experimental.pallas import tpu as pltpu
from jax.sharding import PartitionSpec as P

FRINGE = 128
DISK = 16
LANES = 128
RANK = 12
TILE = 8
HEIGHTS = 2
LAG = 2
SLOTS = LAG + 1

time_step = 0.2
thrust_coef = 1.5

MESH = pl.DeviceIdType.MESH


def slope_matrix(n):
    i = np.arange(n)
    d = (i[:, None] - i[None, :]) % n
    safe = np.where(d == 0, 1, d)
    return np.where(d == 0, 0.0, np.pi / n * (1.0 - 2.0 * (d % 2)) / np.tan(safe * np.pi / n))


def leading(matrix, keep):
    basis = np.linalg.svd(matrix)[2][:keep].T
    signs = np.sign(basis[np.argmax(np.abs(basis), axis=0), np.arange(basis.shape[1])])
    return np.round(basis * signs * 2.0**25) / 2.0**25


def halves(x):
    x = np.asarray(x, np.float32)
    high = x.astype(jnp.bfloat16)
    return np.stack([high, (x - high.astype(np.float32)).astype(jnp.bfloat16)])


def split(x):
    high = x.astype(jnp.bfloat16)
    return high, (x - high.astype(jnp.float32)).astype(jnp.bfloat16)


def mm(a, b):
    return jnp.dot(a, b, preferred_element_type=jnp.float32)


def line_factors(matrix, devices, order):
    width = matrix.shape[0] // devices
    block = lambda a, b: matrix[a * width : (a + 1) * width, b * width : (b + 1) * width]
    own = np.zeros((devices, RANK, width))
    merge = np.zeros((devices, RANK, RANK))
    apply = np.zeros((devices, width, RANK))
    before = None
    for at, here in enumerate(order):
        if before is not None:
            apply[here] = before[:width]
            before = before[width:]
        ahead = order[at + 1 :]
        if not ahead:
            continue
        rows = np.concatenate([np.concatenate([block(a, b) for b in order[: at + 1]], axis=1) for a in ahead], axis=0)
        held = leading(rows.T, RANK)
        own[here] = held.T @ rows[:, at * width :]
        if before is not None:
            merge[here] = held.T @ before
        before = held
    return own, merge, apply


def flow_factors(matrix, devices):
    width = matrix.shape[0] // devices
    rest = RANK - TILE
    place = np.zeros((HEIGHTS, 3 * TILE, RANK))
    for z in range(HEIGHTS):
        place[z, z * TILE : (z + 1) * TILE, :TILE] = np.eye(TILE)
        place[z, 2 * TILE + z * rest : 2 * TILE + (z + 1) * rest, TILE:] = np.eye(rest)
    project = np.zeros((devices, HEIGHTS, 4 * TILE, width))
    merges = np.zeros((devices, 2, 3 * TILE, 3 * TILE))
    applies = np.zeros((devices, HEIGHTS, width, width + 4 * TILE))
    applies[..., :width] = matrix[:width, :width]
    for f, order in enumerate((list(range(devices)), list(range(devices))[::-1])):
        own, merge, apply = line_factors(matrix, devices, order)
        for z in range(HEIGHTS):
            spread = np.concatenate([place[z, z * TILE : (z + 1) * TILE], place[z, 2 * TILE :]], axis=0)
            project[:, z, 2 * f * TILE : 2 * (f + 1) * TILE] = spread @ own
            merges[:, f] += place[z] @ merge @ place[z].T
            applies[:, z, :, width + 2 * f * TILE : width + 2 * (f + 1) * TILE] = apply @ spread.T
    return project, merges, applies


def exchange_kernel(
    sizes, diff_ref, tur_ref, v_hbm, mx_hbm, wp_ref, wm_ref, wy_ref,
    v_scr, inflow_ref, rotor_ref,
    send_r, recv_r, send_l, recv_l, stage, mx_ref, masks, rot_acc, rot_send, rot_recv,
    mx_sem, load_sem, ssem_r, rsem_r, ssem_l, rsem_l, halo_ssem, halo_rsem, flow_ssem, flow_rsem,
    rot_ssem, rot_rsem,
):
    sections, devices, count, lead, hop = sizes
    zb = HEIGHTS
    early = lead - LAG + 1
    _, depth, width, length = v_hbm.shape
    units = depth // zb
    turbines = tur_ref.shape[2]
    section, me, gz = lax.axis_index("sec"), lax.axis_index("gy"), lax.axis_index("gz")
    half = length // 2

    barrier = pltpu.get_barrier_semaphore()
    group = [(dy, dz) for dy in range(devices) for dz in range(count) if (dy, dz) != (0, 0)]
    peer = lambda dy, dz: {"gy": (me + dy) % devices, "gz": (gz + dz) % count}
    for dy, dz in group:
        pl.semaphore_signal(barrier, inc=1, device_id=peer(dy, dz), device_id_type=MESH)
    for ds in range(1, sections):
        pl.semaphore_signal(barrier, inc=1, device_id={"sec": (section + ds) % sections}, device_id_type=MESH)

    backward = (gz + count - 1) // count
    unit_of = lambda i: backward * (units - 1 - i) + (1 - backward) * i
    z_of = lambda i: unit_of(i) * zb

    def load(i):
        z0 = z_of(i)
        return pltpu.make_async_copy(v_hbm.at[:, pl.ds(z0, zb)], v_scr.at[:, pl.ds(z0 + 1, zb)], load_sem.at[i])

    @pl.loop(0, units)
    def _(i):
        load(i).start()

    matrices = pltpu.make_async_copy(mx_hbm, mx_ref, mx_sem)
    matrices.start()

    farm_row = (section + sections - 1) % sections % (sections - 1)
    corner = []
    for k in range(3):
        row = lax.broadcasted_iota(jnp.int32, (turbines, LANES), 0)
        got = jnp.zeros((turbines, LANES), jnp.int32)
        for t in range(turbines):
            got = jnp.where(row == t, tur_ref[farm_row, k, t], got)
        corner.append(got)
    ys = me * width + lax.broadcasted_iota(jnp.int32, (turbines, LANES), 1)
    spans = jnp.where((ys >= corner[1]) & (ys < corner[1] + DISK), 1.0, 0.0)
    masks[...] = jnp.concatenate([spans, jnp.zeros((16 - turbines, LANES), jnp.float32)], axis=0).astype(jnp.bfloat16)
    rot_acc[...] = jnp.zeros_like(rot_acc)

    flows = (
        (me, 1, send_r, recv_r, ssem_r, rsem_r),
        (devices - 1 - me, devices - 1, send_l, recv_l, ssem_l, rsem_l),
    )
    def message(f, i, c):
        _, step, sent, came, ssem, rsem = flows[f]
        return pltpu.make_async_remote_copy(
            sent.at[i, c], came.at[i, c], ssem.at[i, c], rsem.at[i, c],
            device_id={"gy": (me + step) % devices}, device_id_type=MESH,
        )

    def project(i, components=range(3)):
        z0 = z_of(i)
        for c in components:
            rests = []
            for z in range(zb):
                wh, wl = wp_ref[me, z, 0], wp_ref[me, z, 1]
                high, low = split(v_scr[c, z0 + 1 + z])
                if c == 0:
                    tall = jnp.concatenate([wh, masks[:, :width]], axis=0)
                    got = mm(tall, high) + mm(tall, low)
                    zs = gz * depth + z0 + z
                    live = jnp.where((zs >= corner[2]) & (zs < corner[2] + DISK), 1.0, 0.0)
                    for q in range(length // LANES):
                        at = slice(q * LANES, (q + 1) * LANES)
                        rot_acc[:, at] += live * got[4 * TILE : 4 * TILE + turbines, at]
                    got = got[: 4 * TILE] + mm(wl, high)
                else:
                    got = mm(wh, high) + mm(wh, low) + mm(wl, high)
                send_r[i, c, z] = got[:TILE]
                send_l[i, c, z] = got[2 * TILE : 3 * TILE]
                rests.append((got[TILE : 2 * TILE], got[3 * TILE :]))
            send_r[i, c, 2] = rests[0][0] + rests[1][0]
            send_l[i, c, 2] = rests[0][1] + rests[1][1]

    def forward(f, q):
        place, _, sent, came, _, _ = flows[f]
        i, c = q // 3, q % 3

        @pl.when((q >= 0) & (q < 3 * units))
        def _():
            @pl.when(place > 0)
            def _():
                message(f, i, c).wait_recv()

            @pl.when((place > 0) & (place < devices - 1))
            def _():
                high, low = split(came[i, c].reshape(3 * TILE, length))
                wh, wl = wm_ref[me, f, 0], wm_ref[me, f, 1]
                got = mm(wh, high) + mm(wh, low) + mm(wl, high)
                sent[i, c] = sent[i, c] + got.reshape(3, TILE, length)

            @pl.when(place < devices - 1)
            def _():
                message(f, i, c).start()

    def relay(i, k):
        for f in range(2):
            forward(f, 3 * (i + early) + k - hop * flows[f][0])

    def along(i):
        z0, slot = z_of(i), i % SLOTS
        rows = jnp.concatenate([v_scr[c, pl.ds(z0 + 1, zb)].reshape(zb * width, length) for c in range(3)], axis=0)
        wide = mx_ref.shape[-1]
        ahead = pltpu.roll(rows[:, length - wide :], wide - (half - (length - wide)), 1)
        sides = []
        for g, data in enumerate((rows[:, :wide] + ahead, rows[:, :wide] - ahead)):
            high, low = split(data)
            sides.append(mm(high, mx_ref[g, 0]) + mm(low, mx_ref[g, 0]) + mm(high, mx_ref[g, 1]))
        near, far = sides[0] + sides[1], sides[0] - sides[1]
        back = half % LANES
        far = pltpu.roll(far, back, 1)
        cut = half - back
        lane = lax.broadcasted_iota(jnp.int32, (rows.shape[0], LANES), 1)
        seam = jnp.where(lane < back, near[:, cut : cut + LANES], far[:, :LANES])
        slope = jnp.concatenate([near[:, :cut], seam, far[:, LANES : LANES + length - cut - LANES]], axis=1)
        for c in range(3):
            for z in range(zb):
                here = v_scr[c, z0 + 1 + z]
                at = (c * zb + z) * width
                laplace = v_scr[c, z0 + z] + v_scr[c, z0 + 2 + z] - 2.0 * here
                tendency = (1.0 + v_scr[0, z0 + 1 + z]) * slope[at : at + width]
                stage[slot, c, z] = here - time_step * tendency + diff_ref[z0 + z] * laplace

    def across(i):
        z0, slot = z_of(i), i % SLOTS
        for z in range(zb):
            wh, wl = wy_ref[me, z, 0], wy_ref[me, z, 1]
            speed = v_scr[1, z0 + 1 + z]
            for c in range(3):
                parts = [v_scr[c, z0 + 1 + z], recv_r[i, c, z], recv_r[i, c, 2], recv_l[i, c, z], recv_l[i, c, 2]]
                high, low = split(jnp.concatenate(parts, axis=0))
                slope = mm(wh, high) + mm(wh, low) + mm(wl, high)
                v_scr[c, z0 + 1 + z] = stage[slot, c, z] - time_step * (speed * slope)

    up = lambda: pltpu.make_async_remote_copy(
        v_hbm.at[:, depth - 1], v_scr.at[:, 0], halo_ssem.at[0], halo_rsem.at[0],
        device_id={"gz": (gz + 1) % count}, device_id_type=MESH,
    )
    down = lambda: pltpu.make_async_remote_copy(
        v_hbm.at[:, 0], v_scr.at[:, depth + 1], halo_ssem.at[1], halo_rsem.at[1],
        device_id={"gz": (gz + count - 1) % count}, device_id_type=MESH,
    )

    lanes = pl.ds(length - FRINGE, FRINGE)

    def flow(i, to):
        z0 = z_of(i)
        return pltpu.make_async_remote_copy(
            v_scr.at[:, pl.ds(z0 + 1, zb), :, lanes], inflow_ref.at[:, pl.ds(z0, zb)], flow_ssem.at[to - 1, i], flow_rsem.at[i],
            device_id={"sec": to}, device_id_type=MESH,
        )

    def pass_on(i):
        z0 = z_of(i)
        here = inflow_ref.at[:, pl.ds(z0, zb)]
        return pltpu.make_async_remote_copy(
            here, here, flow_ssem.at[0, i], flow_rsem.at[i], device_id={"sec": (section + 1) % sections}, device_id_type=MESH
        )

    direct = [to for to in (1, 2) if to < sections]

    def emit(i):
        @pl.when(section == 0)
        def _():
            for to in direct[::-1]:
                flow(i, to).start()

    def take(i):
        @pl.when(section > 0)
        def _():
            pass_on(i).wait_recv()

        @pl.when((section > 1) & (section < sections - 1))
        def _():
            pass_on(i).start()

    def wait_halo(i):
        @pl.when((unit_of(i) == 0) & (gz > 0))
        def _():
            up().wait_recv()

        @pl.when((unit_of(i) == units - 1) & (gz < count - 1))
        def _():
            down().wait_recv()

    def rotor_sums(i):
        @pl.when(i == units - early)
        def _():
            xs = lax.broadcasted_iota(jnp.int32, (turbines, LANES), 1)
            folded = jnp.zeros((turbines, LANES), jnp.float32)
            for q in range(length // LANES):
                folded = folded + jnp.where(xs + q * LANES == corner[0], rot_acc[:, q * LANES : (q + 1) * LANES], 0.0)
            rot_send[...] = folded

        @pl.when(i == units - early + 1)
        def _():
            for at in range(len(group)):
                rotor(at).start()

    def finish(i):
        across(i)
        emit(i)

        @pl.when(i >= 2)
        def _():
            take(i - 2)

    rotor = lambda at: pltpu.make_async_remote_copy(
        rot_send, rot_recv.at[at], rot_ssem.at[at], rot_rsem.at[at], device_id=peer(*group[at]), device_id_type=MESH
    )

    @pl.when(section == 1)
    def _():
        @pl.loop(0, units)
        def _(i):
            load(i).wait()

        @pl.loop(1, early)
        def _(i):
            project(i)

    @pl.when(section != 1)
    def _():
        load(0).wait()

    for k in range(3):
        project(0, (k,))
        if k == 0:
            pl.semaphore_wait(barrier, len(group) + sections - 1)
        relay(-early, k)

    @pl.when(gz < count - 1)
    def _():
        up().start()

    @pl.when(gz > 0)
    def _():
        down().start()

    @pl.loop(-early + 1, 0)
    def _(i):
        @pl.when(section != 1)
        def _():
            load(i + early).wait()

        for k in range(3):

            @pl.when(section != 1)
            def _():
                project(i + early, (k,))

            relay(i, k)

    @pl.when(gz == 0)
    def _():
        v_scr[:, 0] = jnp.zeros((3, width, length), jnp.float32)

    @pl.when(gz == count - 1)
    def _():
        v_scr[:, depth + 1] = jnp.zeros((3, width, length), jnp.float32)

    for place, _, _, came, _, _ in flows:

        @pl.when(place == 0)
        def _():
            @pl.loop(0, units)
            def _(i):
                came[i] = jnp.zeros(came.shape[1:], jnp.float32)

    matrices.wait()
    @pl.loop(0, units + LAG)
    def _(i):
        @pl.when(i < units - early)
        def _():
            @pl.when(section != 1)
            def _():
                load(i + early).wait()

            project(i + early)

        relay(i, 0)

        @pl.when(i < units)
        def _():
            wait_halo(i)
            along(i)

        rotor_sums(i)
        relay(i, 1)

        @pl.when(i >= LAG)
        def _():
            finish(i - LAG)

        relay(i, 2)

    total = rot_send[...]
    for at in range(len(group)):
        rotor(at).wait()
        total = total + rot_recv[at]
    rotor_ref[...] = total

    @pl.when(gz < count - 1)
    def _():
        up().wait_send()

    @pl.when(gz > 0)
    def _():
        down().wait_send()

    for f in range(2):

        @pl.when(flows[f][0] < devices - 1)
        def _():
            @pl.loop(0, units)
            def _(i):
                for c in range(3):
                    message(f, i, c).wait_send()

    @pl.when(section == 0)
    def _():
        @pl.loop(0, units)
        def _(i):
            for to in direct:
                flow(i, to).wait_send()

    @pl.loop(units - 2, units)
    def _(i):
        take(i)

    @pl.when((section > 1) & (section < sections - 1))
    def _():
        @pl.loop(0, units)
        def _(i):
            pass_on(i).wait_send()


def finish_kernel(sections, tur_ref, start_ref, _, inflow_ref, rotor_ref, out_hbm, v_ref, sems):
    section, me, gz = lax.axis_index("sec"), lax.axis_index("gy"), lax.axis_index("gz")
    _, depth, width, length = out_hbm.shape
    zb = depth // sems.shape[0]
    farm = (section + sections - 1) % sections % (sections - 1)

    def store(i):
        z0 = i * zb
        return pltpu.make_async_copy(v_ref.at[:, pl.ds(z0 + 1, zb)], out_hbm.at[:, pl.ds(z0, zb)], sems.at[i])

    @pl.when(section == 0)
    def _():
        @pl.loop(0, depth // zb)
        def _(i):
            store(i).start()

    @pl.when(section > 0)
    def _():
        speed = 1.0 + jnp.sum(rotor_ref[...], axis=1, keepdims=True) / (DISK * DISK)
        push = jnp.broadcast_to(time_step * (-0.5 * thrust_coef * speed * jnp.abs(speed)), rotor_ref.shape)
        start = start_ref[farm]
        turn = lax.rem(start, LANES)
        offset = lax.broadcasted_iota(jnp.int32, (16, LANES), 0) // 8 * LANES - turn
        offset = offset + lax.broadcasted_iota(jnp.int32, (16, LANES), 1)
        inside = (offset >= 0) & (offset < FRINGE)
        weights = jnp.where(inside, jnp.sin(jnp.pi * (offset.astype(jnp.float32) + 0.5) / FRINGE) ** 2, 0.0)

        @pl.loop(0, depth // zb)
        def _(i):
            y0, here0 = me * width, i * zb
            z0 = gz * depth + here0
            for t in range(tur_ref.shape[2]):
                tx, ty, tz = (tur_ref[farm, k, t] for k in range(3))

                @pl.when((tz < z0 + zb) & (tz + DISK > z0) & (ty < y0 + width) & (ty + DISK > y0))
                def _():
                    at = pl.ds(pl.multiple_of(tx // LANES * LANES, LANES), LANES)
                    shape = (width, LANES)
                    ys = y0 + lax.broadcasted_iota(jnp.int32, shape, 0)
                    xs = tx // LANES * LANES + lax.broadcasted_iota(jnp.int32, shape, 1)
                    disk = (xs == tx) & (ys >= ty) & (ys < ty + DISK)
                    for z in range(zb):
                        hit = disk & (z0 + z >= tz) & (z0 + z < tz + DISK)
                        v_ref[0, here0 + z + 1, :, at] = v_ref[0, here0 + z + 1, :, at] + jnp.where(hit, push[t : t + 1], 0.0)

            for j in range(2):

                @pl.when(start // LANES + j < length // LANES)
                def _():
                    at = pl.ds(pl.multiple_of((start // LANES + j) * LANES, LANES), LANES)
                    weight = weights[8 * j : 8 * j + 1]
                    for c in range(3):
                        for z in range(zb):
                            here = v_ref[c, here0 + z + 1, :, at]
                            flown = pltpu.roll(inflow_ref[c, here0 + z], turn, 1)
                            v_ref[c, here0 + z + 1, :, at] = here + weight * (flown - here)

            store(i).start()

    @pl.loop(0, depth // zb)
    def _(i):
        store(i).wait()


def cost(flops, bytes_accessed):
    return pl.CostEstimate(flops=int(flops), bytes_accessed=int(bytes_accessed), transcendentals=0)


def body(velocity, diffusion, turbines, fringe_start):
    current = velocity[0]
    _, depth, width, length = current.shape
    sections, devices, count = (lax.axis_size(a) for a in ("sec", "gy", "gz"))
    f32, bf16 = jnp.float32, jnp.bfloat16
    units = depth // HEIGHTS
    hop = max(1, 9 // (devices - 1))
    lead = -(-hop * (devices - 1) // 3)
    rows = 3 * depth
    half = length // 2
    wide = -(-half // LANES) * LANES
    number = turbines.shape[1]
    turbines = jnp.swapaxes(turbines, 1, 2)

    straight = slope_matrix(length)
    mx = np.zeros((2, wide, wide))
    mx[0, :half, :half] = 0.5 * (straight[:half, :half] + straight[:half, half:]).T
    mx[1, :half, :half] = 0.5 * (straight[:half, :half] - straight[:half, half:]).T
    factors = flow_factors(slope_matrix(width * devices), devices)
    pair = lambda x: np.moveaxis(halves(x), 0, -3)
    consts = [jnp.asarray(pair(x)) for x in (mx, *factors)]

    vmem = pl.BlockSpec(memory_space=pltpu.VMEM)
    smem = pl.BlockSpec(memory_space=pltpu.SMEM)
    hbm = pl.BlockSpec(memory_space=pl.ANY)
    message = pltpu.VMEM((units, 3, 3, TILE, length), f32)
    dma = pltpu.SemaphoreType.DMA
    others = devices * count - 1
    advanced, inflow, rotor = pl.pallas_call(
        functools.partial(exchange_kernel, (sections, devices, count, lead, hop)),
        out_shape=(
            pltpu.VMEM((3, depth + 2, width, length), f32),
            pltpu.VMEM((3, depth, width, FRINGE), f32),
            pltpu.VMEM((number, LANES), f32),
        ),
        in_specs=[smem, smem, hbm, hbm, vmem, vmem, vmem],
        out_specs=(vmem, vmem, vmem),
        scratch_shapes=[
            message, message, message, message,
            pltpu.VMEM((SLOTS, 3, HEIGHTS, width, length), f32),
            pltpu.VMEM(consts[0].shape, bf16),
            pltpu.VMEM((16, LANES), bf16),
            pltpu.VMEM((number, length), f32),
            pltpu.VMEM((number, LANES), f32),
            pltpu.VMEM((others, number, LANES), f32),
            dma, dma((units,)), dma((units, 3)), dma((units, 3)), dma((units, 3)), dma((units, 3)), dma((2,)), dma((2,)),
            dma((2, units)), dma((units,)), dma((others,)), dma((others,)),
        ],
        compiler_params=pltpu.CompilerParams(collective_id=0, has_side_effects=True, vmem_limit_bytes=30 * 1024 * 1024),
        cost_estimate=cost(6 * rows * width * length * length, 12 * rows * width * length),
        name="exchange",
    )(diffusion, turbines, current, *consts)

    chip = lambda x: pltpu.with_memory_space_constraint(x, pltpu.VMEM)
    out, _ = pl.pallas_call(
        functools.partial(finish_kernel, sections),
        out_shape=(jax.ShapeDtypeStruct(current.shape, f32), pltpu.VMEM((3, depth + 2, width, length), f32)),
        in_specs=[smem, smem, vmem, vmem, vmem],
        out_specs=(hbm, vmem),
        scratch_shapes=[dma((depth // min(4, depth),))],
        input_output_aliases={2: 1},
        compiler_params=pltpu.CompilerParams(vmem_limit_bytes=30 * 1024 * 1024),
        cost_estimate=cost(rows * width * length, 8 * rows * width * length),
        name="finish",
    )(turbines, fringe_start, chip(advanced), chip(inflow), chip(rotor))
    return out[None]


def solution(mesh):
    in_specs = (P("sec", None, "gz", "gy", None), P("gz"), P(), P())
    out_specs = P("sec", None, "gz", "gy", None)
    return jax.shard_map(body, mesh=mesh, in_specs=in_specs, out_specs=out_specs, check_vma=False)
```

```python
import functools

import jax
import jax.numpy as jnp
import numpy as np
from jax import lax
from jax.experimental import pallas as pl
from jax.experimental.pallas import tpu as pltpu
from jax.sharding import PartitionSpec as P

FRINGE = 128
DISK = 16
LANES = 128
RANK = 12
TILE = 8
HEIGHTS = 2
LAG = 2
SLOTS = LAG + 1

time_step = 0.2
thrust_coef = 1.5

MESH = pl.DeviceIdType.MESH


def slope_matrix(n):
    i = np.arange(n)
    d = (i[:, None] - i[None, :]) % n
    safe = np.where(d == 0, 1, d)
    return np.where(d == 0, 0.0, np.pi / n * (1.0 - 2.0 * (d % 2)) / np.tan(safe * np.pi / n))


def leading(matrix, keep):
    basis = np.linalg.svd(matrix)[2][:keep].T
    signs = np.sign(basis[np.argmax(np.abs(basis), axis=0), np.arange(basis.shape[1])])
    return np.round(basis * signs * 2.0**25) / 2.0**25


def halves(x):
    x = np.asarray(x, np.float32)
    high = x.astype(jnp.bfloat16)
    return np.stack([high, (x - high.astype(np.float32)).astype(jnp.bfloat16)])


def split(x):
    high = x.astype(jnp.bfloat16)
    return high, (x - high.astype(jnp.float32)).astype(jnp.bfloat16)


def mm(a, b):
    return jnp.dot(a, b, preferred_element_type=jnp.float32)


def line_factors(matrix, devices, order):
    width = matrix.shape[0] // devices
    block = lambda a, b: matrix[a * width : (a + 1) * width, b * width : (b + 1) * width]
    own = np.zeros((devices, RANK, width))
    merge = np.zeros((devices, RANK, RANK))
    apply = np.zeros((devices, width, RANK))
    before = None
    for at, here in enumerate(order):
        if before is not None:
            apply[here] = before[:width]
            before = before[width:]
        ahead = order[at + 1 :]
        if not ahead:
            continue
        rows = np.concatenate([np.concatenate([block(a, b) for b in order[: at + 1]], axis=1) for a in ahead], axis=0)
        held = leading(rows.T, RANK)
        own[here] = held.T @ rows[:, at * width :]
        if before is not None:
            merge[here] = held.T @ before
        before = held
    return own, merge, apply


def flow_factors(matrix, devices):
    width = matrix.shape[0] // devices
    rest = RANK - TILE
    place = np.zeros((HEIGHTS, 3 * TILE, RANK))
    for z in range(HEIGHTS):
        place[z, z * TILE : (z + 1) * TILE, :TILE] = np.eye(TILE)
        place[z, 2 * TILE + z * rest : 2 * TILE + (z + 1) * rest, TILE:] = np.eye(rest)
    project = np.zeros((devices, HEIGHTS, 4 * TILE, width))
    merges = np.zeros((devices, 2, 3 * TILE, 3 * TILE))
    applies = np.zeros((devices, HEIGHTS, width, width + 4 * TILE))
    applies[..., :width] = matrix[:width, :width]
    for f, order in enumerate((list(range(devices)), list(range(devices))[::-1])):
        own, merge, apply = line_factors(matrix, devices, order)
        for z in range(HEIGHTS):
            spread = np.concatenate([place[z, z * TILE : (z + 1) * TILE], place[z, 2 * TILE :]], axis=0)
            project[:, z, 2 * f * TILE : 2 * (f + 1) * TILE] = spread @ own
            merges[:, f] += place[z] @ merge @ place[z].T
            applies[:, z, :, width + 2 * f * TILE : width + 2 * (f + 1) * TILE] = apply @ spread.T
    return project, merges, applies


def exchange_kernel(
    sizes, diff_ref, tur_ref, v_hbm, mx_hbm, wp_ref, wm_ref, wy_ref,
    v_scr, inflow_ref, rotor_ref,
    send_r, recv_r, send_l, recv_l, stage, mx_ref, masks, rot_acc, rot_send, rot_recv,
    mx_sem, load_sem, ssem_r, rsem_r, ssem_l, rsem_l, halo_ssem, halo_rsem, flow_ssem, flow_rsem,
    rot_ssem, rot_rsem,
):
    sections, devices, count, lead, hop = sizes
    zb = HEIGHTS
    early = lead - LAG + 1
    _, depth, width, length = v_hbm.shape
    units = depth // zb
    turbines = tur_ref.shape[2]
    section, me, gz = lax.axis_index("sec"), lax.axis_index("gy"), lax.axis_index("gz")
    half = length // 2

    barrier = pltpu.get_barrier_semaphore()
    group = [(dy, dz) for dy in range(devices) for dz in range(count) if (dy, dz) != (0, 0)]
    peer = lambda dy, dz: {"gy": (me + dy) % devices, "gz": (gz + dz) % count}
    for dy, dz in group:
        pl.semaphore_signal(barrier, inc=1, device_id=peer(dy, dz), device_id_type=MESH)
    for ds in range(1, sections):
        pl.semaphore_signal(barrier, inc=1, device_id={"sec": (section + ds) % sections}, device_id_type=MESH)

    backward = (gz + count - 1) // count
    unit_of = lambda i: backward * (units - 1 - i) + (1 - backward) * i
    z_of = lambda i: unit_of(i) * zb

    def load(i):
        z0 = z_of(i)
        return pltpu.make_async_copy(v_hbm.at[:, pl.ds(z0, zb)], v_scr.at[:, pl.ds(z0 + 1, zb)], load_sem.at[i])

    @pl.loop(0, units)
    def _(i):
        load(i).start()

    matrices = pltpu.make_async_copy(mx_hbm, mx_ref, mx_sem)
    matrices.start()

    farm_row = (section + sections - 1) % sections % (sections - 1)
    corner = []
    for k in range(3):
        row = lax.broadcasted_iota(jnp.int32, (turbines, LANES), 0)
        got = jnp.zeros((turbines, LANES), jnp.int32)
        for t in range(turbines):
            got = jnp.where(row == t, tur_ref[farm_row, k, t], got)
        corner.append(got)
    ys = me * width + lax.broadcasted_iota(jnp.int32, (turbines, LANES), 1)
    spans = jnp.where((ys >= corner[1]) & (ys < corner[1] + DISK), 1.0, 0.0)
    masks[...] = jnp.concatenate([spans, jnp.zeros((16 - turbines, LANES), jnp.float32)], axis=0).astype(jnp.bfloat16)
    rot_acc[...] = jnp.zeros_like(rot_acc)

    flows = (
        (me, 1, send_r, recv_r, ssem_r, rsem_r),
        (devices - 1 - me, devices - 1, send_l, recv_l, ssem_l, rsem_l),
    )
    def message(f, i, c):
        _, step, sent, came, ssem, rsem = flows[f]
        return pltpu.make_async_remote_copy(
            sent.at[i, c], came.at[i, c], ssem.at[i, c], rsem.at[i, c],
            device_id={"gy": (me + step) % devices}, device_id_type=MESH,
        )

    def project(i, components=range(3)):
        z0 = z_of(i)
        for c in components:
            rests = []
            for z in range(zb):
                wh, wl = wp_ref[me, z, 0], wp_ref[me, z, 1]
                high, low = split(v_scr[c, z0 + 1 + z])
                if c == 0:
                    tall = jnp.concatenate([wh, masks[:, :width]], axis=0)
                    got = mm(tall, high) + mm(tall, low)
                    zs = gz * depth + z0 + z
                    live = jnp.where((zs >= corner[2]) & (zs < corner[2] + DISK), 1.0, 0.0)
                    for q in range(length // LANES):
                        at = slice(q * LANES, (q + 1) * LANES)
                        rot_acc[:, at] += live * got[4 * TILE : 4 * TILE + turbines, at]
                    got = got[: 4 * TILE] + mm(wl, high)
                else:
                    got = mm(wh, high) + mm(wh, low) + mm(wl, high)
                send_r[i, c, z] = got[:TILE]
                send_l[i, c, z] = got[2 * TILE : 3 * TILE]
                rests.append((got[TILE : 2 * TILE], got[3 * TILE :]))
            send_r[i, c, 2] = rests[0][0] + rests[1][0]
            send_l[i, c, 2] = rests[0][1] + rests[1][1]

    def forward(f, q):
        place, _, sent, came, _, _ = flows[f]
        i, c = q // 3, q % 3

        @pl.when((q >= 0) & (q < 3 * units))
        def _():
            @pl.when(place > 0)
            def _():
                message(f, i, c).wait_recv()

            @pl.when((place > 0) & (place < devices - 1))
            def _():
                high, low = split(came[i, c].reshape(3 * TILE, length))
                wh, wl = wm_ref[me, f, 0], wm_ref[me, f, 1]
                got = mm(wh, high) + mm(wh, low) + mm(wl, high)
                sent[i, c] = sent[i, c] + got.reshape(3, TILE, length)

            @pl.when(place < devices - 1)
            def _():
                message(f, i, c).start()

    def relay(i, k):
        @pl.when(2 * me < devices)
        def _():
            for f in (0, 1):
                forward(f, 3 * (i + early) + k - hop * flows[f][0])

        @pl.when(2 * me >= devices)
        def _():
            for f in (1, 0):
                forward(f, 3 * (i + early) + k - hop * flows[f][0])

    def along(i):
        z0, slot = z_of(i), i % SLOTS
        rows = jnp.concatenate([v_scr[c, pl.ds(z0 + 1, zb)].reshape(zb * width, length) for c in range(3)], axis=0)
        wide = mx_ref.shape[-1]
        ahead = pltpu.roll(rows[:, length - wide :], wide - (half - (length - wide)), 1)
        sides = []
        for g, data in enumerate((rows[:, :wide] + ahead, rows[:, :wide] - ahead)):
            high, low = split(data)
            sides.append(mm(high, mx_ref[g, 0]) + mm(low, mx_ref[g, 0]) + mm(high, mx_ref[g, 1]))
        near, far = sides[0] + sides[1], sides[0] - sides[1]
        back = half % LANES
        far = pltpu.roll(far, back, 1)
        cut = half - back
        lane = lax.broadcasted_iota(jnp.int32, (rows.shape[0], LANES), 1)
        seam = jnp.where(lane < back, near[:, cut : cut + LANES], far[:, :LANES])
        slope = jnp.concatenate([near[:, :cut], seam, far[:, LANES : LANES + length - cut - LANES]], axis=1)
        for c in range(3):
            for z in range(zb):
                here = v_scr[c, z0 + 1 + z]
                at = (c * zb + z) * width
                laplace = v_scr[c, z0 + z] + v_scr[c, z0 + 2 + z] - 2.0 * here
                tendency = (1.0 + v_scr[0, z0 + 1 + z]) * slope[at : at + width]
                stage[slot, c, z] = here - time_step * tendency + diff_ref[z0 + z] * laplace

    def across(i):
        z0, slot = z_of(i), i % SLOTS
        for z in range(zb):
            wh, wl = wy_ref[me, z, 0], wy_ref[me, z, 1]
            speed = v_scr[1, z0 + 1 + z]
            for c in range(3):
                parts = [v_scr[c, z0 + 1 + z], recv_r[i, c, z], recv_r[i, c, 2], recv_l[i, c, z], recv_l[i, c, 2]]
                high, low = split(jnp.concatenate(parts, axis=0))
                slope = mm(wh, high) + mm(wh, low) + mm(wl, high)
                v_scr[c, z0 + 1 + z] = stage[slot, c, z] - time_step * (speed * slope)

    up = lambda: pltpu.make_async_remote_copy(
        v_hbm.at[:, depth - 1], v_scr.at[:, 0], halo_ssem.at[0], halo_rsem.at[0],
        device_id={"gz": (gz + 1) % count}, device_id_type=MESH,
    )
    down = lambda: pltpu.make_async_remote_copy(
        v_hbm.at[:, 0], v_scr.at[:, depth + 1], halo_ssem.at[1], halo_rsem.at[1],
        device_id={"gz": (gz + count - 1) % count}, device_id_type=MESH,
    )

    lanes = pl.ds(length - FRINGE, FRINGE)

    def flow(i, to):
        z0 = z_of(i)
        return pltpu.make_async_remote_copy(
            v_scr.at[:, pl.ds(z0 + 1, zb), :, lanes], inflow_ref.at[:, pl.ds(z0, zb)], flow_ssem.at[to - 1, i], flow_rsem.at[i],
            device_id={"sec": to}, device_id_type=MESH,
        )

    def pass_on(i):
        z0 = z_of(i)
        here = inflow_ref.at[:, pl.ds(z0, zb)]
        return pltpu.make_async_remote_copy(
            here, here, flow_ssem.at[0, i], flow_rsem.at[i], device_id={"sec": (section + 1) % sections}, device_id_type=MESH
        )

    direct = [to for to in (1, 2) if to < sections]

    def emit(i):
        @pl.when(section == 0)
        def _():
            for to in direct[::-1]:
                flow(i, to).start()

    def take(i):
        @pl.when(section > 0)
        def _():
            pass_on(i).wait_recv()

        @pl.when((section > 1) & (section < sections - 1))
        def _():
            pass_on(i).start()

    def wait_halo(i):
        @pl.when((unit_of(i) == 0) & (gz > 0))
        def _():
            up().wait_recv()

        @pl.when((unit_of(i) == units - 1) & (gz < count - 1))
        def _():
            down().wait_recv()

    def rotor_sums(i):
        @pl.when(i == units - early)
        def _():
            xs = lax.broadcasted_iota(jnp.int32, (turbines, LANES), 1)
            folded = jnp.zeros((turbines, LANES), jnp.float32)
            for q in range(length // LANES):
                folded = folded + jnp.where(xs + q * LANES == corner[0], rot_acc[:, q * LANES : (q + 1) * LANES], 0.0)
            rot_send[...] = folded

        @pl.when(i == units - early + 1)
        def _():
            for at in range(len(group)):
                rotor(at).start()

    def finish(i):
        across(i)
        emit(i)

        @pl.when(i >= 2)
        def _():
            take(i - 2)

    rotor = lambda at: pltpu.make_async_remote_copy(
        rot_send, rot_recv.at[at], rot_ssem.at[at], rot_rsem.at[at], device_id=peer(*group[at]), device_id_type=MESH
    )

    @pl.when(section == 1)
    def _():
        @pl.loop(0, units)
        def _(i):
            load(i).wait()

        @pl.loop(1, early)
        def _(i):
            project(i)

    @pl.when(section != 1)
    def _():
        load(0).wait()

    for k in range(3):
        project(0, (k,))
        if k == 0:
            pl.semaphore_wait(barrier, len(group) + sections - 1)
        relay(-early, k)

    @pl.when(gz < count - 1)
    def _():
        up().start()

    @pl.when(gz > 0)
    def _():
        down().start()

    @pl.loop(-early + 1, 0)
    def _(i):
        @pl.when(section != 1)
        def _():
            load(i + early).wait()

        for k in range(3):

            @pl.when(section != 1)
            def _():
                project(i + early, (k,))

            relay(i, k)

    @pl.when(gz == 0)
    def _():
        v_scr[:, 0] = jnp.zeros((3, width, length), jnp.float32)

    @pl.when(gz == count - 1)
    def _():
        v_scr[:, depth + 1] = jnp.zeros((3, width, length), jnp.float32)

    for place, _, _, came, _, _ in flows:

        @pl.when(place == 0)
        def _():
            @pl.loop(0, units)
            def _(i):
                came[i] = jnp.zeros(came.shape[1:], jnp.float32)

    matrices.wait()
    @pl.loop(0, units + LAG)
    def _(i):
        @pl.when(i < units - early)
        def _():
            @pl.when(section != 1)
            def _():
                load(i + early).wait()

            project(i + early)

        relay(i, 0)

        @pl.when(i < units)
        def _():
            wait_halo(i)
            along(i)

        rotor_sums(i)
        relay(i, 1)

        @pl.when(i >= LAG)
        def _():
            finish(i - LAG)

        relay(i, 2)

    total = rot_send[...]
    for at in range(len(group)):
        rotor(at).wait()
        total = total + rot_recv[at]
    rotor_ref[...] = total

    @pl.when(gz < count - 1)
    def _():
        up().wait_send()

    @pl.when(gz > 0)
    def _():
        down().wait_send()

    for f in range(2):

        @pl.when(flows[f][0] < devices - 1)
        def _():
            @pl.loop(0, units)
            def _(i):
                for c in range(3):
                    message(f, i, c).wait_send()

    @pl.when(section == 0)
    def _():
        @pl.loop(0, units)
        def _(i):
            for to in direct:
                flow(i, to).wait_send()

    @pl.loop(units - 2, units)
    def _(i):
        take(i)

    @pl.when((section > 1) & (section < sections - 1))
    def _():
        @pl.loop(0, units)
        def _(i):
            pass_on(i).wait_send()


def finish_kernel(sections, tur_ref, start_ref, _, inflow_ref, rotor_ref, out_hbm, v_ref, sems):
    section, me, gz = lax.axis_index("sec"), lax.axis_index("gy"), lax.axis_index("gz")
    _, depth, width, length = out_hbm.shape
    zb = depth // sems.shape[0]
    farm = (section + sections - 1) % sections % (sections - 1)

    def store(i):
        z0 = i * zb
        return pltpu.make_async_copy(v_ref.at[:, pl.ds(z0 + 1, zb)], out_hbm.at[:, pl.ds(z0, zb)], sems.at[i])

    @pl.when(section == 0)
    def _():
        @pl.loop(0, depth // zb)
        def _(i):
            store(i).start()

    @pl.when(section > 0)
    def _():
        speed = 1.0 + jnp.sum(rotor_ref[...], axis=1, keepdims=True) / (DISK * DISK)
        push = jnp.broadcast_to(time_step * (-0.5 * thrust_coef * speed * jnp.abs(speed)), rotor_ref.shape)
        start = start_ref[farm]
        turn = lax.rem(start, LANES)
        offset = lax.broadcasted_iota(jnp.int32, (16, LANES), 0) // 8 * LANES - turn
        offset = offset + lax.broadcasted_iota(jnp.int32, (16, LANES), 1)
        inside = (offset >= 0) & (offset < FRINGE)
        weights = jnp.where(inside, jnp.sin(jnp.pi * (offset.astype(jnp.float32) + 0.5) / FRINGE) ** 2, 0.0)

        @pl.loop(0, depth // zb)
        def _(i):
            y0, here0 = me * width, i * zb
            z0 = gz * depth + here0
            for t in range(tur_ref.shape[2]):
                tx, ty, tz = (tur_ref[farm, k, t] for k in range(3))

                @pl.when((tz < z0 + zb) & (tz + DISK > z0) & (ty < y0 + width) & (ty + DISK > y0))
                def _():
                    at = pl.ds(pl.multiple_of(tx // LANES * LANES, LANES), LANES)
                    shape = (width, LANES)
                    ys = y0 + lax.broadcasted_iota(jnp.int32, shape, 0)
                    xs = tx // LANES * LANES + lax.broadcasted_iota(jnp.int32, shape, 1)
                    disk = (xs == tx) & (ys >= ty) & (ys < ty + DISK)
                    for z in range(zb):
                        hit = disk & (z0 + z >= tz) & (z0 + z < tz + DISK)
                        v_ref[0, here0 + z + 1, :, at] = v_ref[0, here0 + z + 1, :, at] + jnp.where(hit, push[t : t + 1], 0.0)

            for j in range(2):

                @pl.when(start // LANES + j < length // LANES)
                def _():
                    at = pl.ds(pl.multiple_of((start // LANES + j) * LANES, LANES), LANES)
                    weight = weights[8 * j : 8 * j + 1]
                    for c in range(3):
                        for z in range(zb):
                            here = v_ref[c, here0 + z + 1, :, at]
                            flown = pltpu.roll(inflow_ref[c, here0 + z], turn, 1)
                            v_ref[c, here0 + z + 1, :, at] = here + weight * (flown - here)

            store(i).start()

    @pl.loop(0, depth // zb)
    def _(i):
        store(i).wait()


def cost(flops, bytes_accessed):
    return pl.CostEstimate(flops=int(flops), bytes_accessed=int(bytes_accessed), transcendentals=0)


def body(velocity, diffusion, turbines, fringe_start):
    current = velocity[0]
    _, depth, width, length = current.shape
    sections, devices, count = (lax.axis_size(a) for a in ("sec", "gy", "gz"))
    f32, bf16 = jnp.float32, jnp.bfloat16
    units = depth // HEIGHTS
    hop = max(1, 9 // (devices - 1))
    lead = -(-hop * (devices - 1) // 3)
    rows = 3 * depth
    half = length // 2
    wide = -(-half // LANES) * LANES
    number = turbines.shape[1]
    turbines = jnp.swapaxes(turbines, 1, 2)

    straight = slope_matrix(length)
    mx = np.zeros((2, wide, wide))
    mx[0, :half, :half] = 0.5 * (straight[:half, :half] + straight[:half, half:]).T
    mx[1, :half, :half] = 0.5 * (straight[:half, :half] - straight[:half, half:]).T
    factors = flow_factors(slope_matrix(width * devices), devices)
    pair = lambda x: np.moveaxis(halves(x), 0, -3)
    consts = [jnp.asarray(pair(x)) for x in (mx, *factors)]

    vmem = pl.BlockSpec(memory_space=pltpu.VMEM)
    smem = pl.BlockSpec(memory_space=pltpu.SMEM)
    hbm = pl.BlockSpec(memory_space=pl.ANY)
    message = pltpu.VMEM((units, 3, 3, TILE, length), f32)
    dma = pltpu.SemaphoreType.DMA
    others = devices * count - 1
    advanced, inflow, rotor = pl.pallas_call(
        functools.partial(exchange_kernel, (sections, devices, count, lead, hop)),
        out_shape=(
            pltpu.VMEM((3, depth + 2, width, length), f32),
            pltpu.VMEM((3, depth, width, FRINGE), f32),
            pltpu.VMEM((number, LANES), f32),
        ),
        in_specs=[smem, smem, hbm, hbm, vmem, vmem, vmem],
        out_specs=(vmem, vmem, vmem),
        scratch_shapes=[
            message, message, message, message,
            pltpu.VMEM((SLOTS, 3, HEIGHTS, width, length), f32),
            pltpu.VMEM(consts[0].shape, bf16),
            pltpu.VMEM((16, LANES), bf16),
            pltpu.VMEM((number, length), f32),
            pltpu.VMEM((number, LANES), f32),
            pltpu.VMEM((others, number, LANES), f32),
            dma, dma((units,)), dma((units, 3)), dma((units, 3)), dma((units, 3)), dma((units, 3)), dma((2,)), dma((2,)),
            dma((2, units)), dma((units,)), dma((others,)), dma((others,)),
        ],
        compiler_params=pltpu.CompilerParams(collective_id=0, has_side_effects=True, vmem_limit_bytes=30 * 1024 * 1024),
        cost_estimate=cost(6 * rows * width * length * length, 12 * rows * width * length),
        name="exchange",
    )(diffusion, turbines, current, *consts)

    chip = lambda x: pltpu.with_memory_space_constraint(x, pltpu.VMEM)
    out, _ = pl.pallas_call(
        functools.partial(finish_kernel, sections),
        out_shape=(jax.ShapeDtypeStruct(current.shape, f32), pltpu.VMEM((3, depth + 2, width, length), f32)),
        in_specs=[smem, smem, vmem, vmem, vmem],
        out_specs=(hbm, vmem),
        scratch_shapes=[dma((depth // min(4, depth),))],
        input_output_aliases={2: 1},
        compiler_params=pltpu.CompilerParams(vmem_limit_bytes=30 * 1024 * 1024),
        cost_estimate=cost(rows * width * length, 8 * rows * width * length),
        name="finish",
    )(turbines, fringe_start, chip(advanced), chip(inflow), chip(rotor))
    return out[None]


def solution(mesh):
    in_specs = (P("sec", None, "gz", "gy", None), P("gz"), P(), P())
    out_specs = P("sec", None, "gz", "gy", None)
    return jax.shard_map(body, mesh=mesh, in_specs=in_specs, out_specs=out_specs, check_vma=False)
```
